32 devices in a mesh: req: 8 (over z, y), tp: 4 (over x, core).
Axes of the slice: x: 2, y: 2, z: 4, core: 2. Of those that a mesh axis runs over, the one named last changes fastest.
Arguments:
- tokens: bfloat16 [4096, 2048], P('req', 'tp'), may hold values from -6 to 6
- owners: int32 [8], replicated, may hold values from 0 to 7, each once
- request_groups: int32 [8, 2], P('req'), may hold values from 0 to 3, all different within a row
- request_lengths: int32 [8, 2], P('req'), may hold values from 64 to 448, as said below
- prefix_cache: bfloat16 [8, 2, 768, 320], P('req'), may hold values from -25 to 25
- attn_gain: float32 [2048], replicated, may hold values from 0.5 to 1.5
- query_weight: bfloat16 [2048, 1280], P(None, 'tp'), may hold values from -0.125 to 0.125
- key_value_weight: bfloat16 [2048, 640], replicated, may hold values from -0.125 to 0.125
- query_gain: float32 [64], replicated, may hold values from 0.7 to 6
- key_gain: float32 [64], replicated, may hold values from 0.7 to 6
- w_out: bfloat16 [1280, 2048], P('tp'), may hold values from -0.15625 to 0.15625
- ffn_gain: float32 [2048], replicated, may hold values from 0.5 to 1.5
- w_gate_up: bfloat16 [2048, 2, 5120], P(None, None, 'tp'), may hold values from -0.125 to 0.125
- w_down: bfloat16 [5120, 2048], P('tp'), may hold values from -0.078125 to 0.078125
Outputs:
- hidden: bfloat16 [4096, 2048], P('req', 'tp')
- suffix_cache: bfloat16 [4096, 2, 320], P('req')
The draws below stay inside these ranges and needn't reach their ends.
Inputs may be any that keep to these rules, and one draw needn't show every extreme that they name: `owners`: every req index holds exactly one half of one group's prefix. `request_groups`: the two groups of one device differ; every group has a request. `request_lengths`: a device's two lengths sum to 512.
All inputs are finite; a program needn't handle non-finite values.
Results may differ from the reference program's by a relative error of at most 0.012.
The reference program's roundings to bfloat16 on the way count: a program that leaves them out, or rounds other values in their place, can miss the bound.
Values may be sent and summed in bfloat16 or wider, within the bound.
No kernel may reach another device: no remote copies, remote signals or barrier semaphores. Data moves between devices by JAX's collectives and lax.ppermute only.
A program may use at most 192 MiB of HBM per device.

```python
import math
import jax
import jax.numpy as jnp
from jax import lax

MODEL_WIDTH = 2048
HQ = 20
KEY_VALUE_HEADS = 5
HEAD_SIZE = 64
FF = 5120
PREFIX = 1536
SUFFIX_TOKENS = 512
MAXLEN = 448
PREFIX_HALF_LEN = 768
GROUPS = 4
TOKENS = 4096
N_REQ = 8
N_TP = 4


def draw_request_lengths(key, part):
    first_len = jax.random.randint(key, (N_REQ,), SUFFIX_TOKENS - MAXLEN, MAXLEN + 1)
    first_len = jnp.where(jnp.arange(N_REQ) == 0, MAXLEN, first_len).astype(jnp.int32)
    return jnp.stack([first_len, SUFFIX_TOKENS - first_len], axis=1).astype(jnp.int32)


def draw_prefix_cache(key, part):
    key_seed, value_seed = jax.random.split(jax.random.fold_in(key, 7))
    tensor_shape = (N_REQ, 1, PREFIX_HALF_LEN, KEY_VALUE_HEADS * HEAD_SIZE)
    key_rows = jnp.clip(jax.random.normal(key_seed, tensor_shape, jnp.float32), -6.0, 6.0)
    value_rows = jnp.clip(jax.random.normal(value_seed, tensor_shape, jnp.float32), -6.0, 6.0)
    return jnp.concatenate([key_rows, value_rows], axis=1).astype(jnp.bfloat16)


def head_gain(gain_seed):
    return jnp.exp(jax.random.uniform(gain_seed, (HEAD_SIZE,), jnp.float32, math.log(0.7), math.log(1.4)))


def draw_query_gain(key, part):
    return head_gain(jax.random.fold_in(key, 11))


def draw_key_gain(key, part):
    return head_gain(jax.random.fold_in(key, 23))


def shard_levels(stream_key, dims, cuts, least, largest):
    loudness, own = 1.0, jax.random.fold_in(stream_key, 6)
    for axis_at, shards_of in cuts:
        heights = jnp.exp(jax.random.uniform(jax.random.fold_in(own, axis_at), (shards_of,), jnp.float32, least / len(cuts), largest / len(cuts)))
        loudness = loudness * jnp.repeat(heights, dims[axis_at] // shards_of).reshape([-1 if axis == axis_at else 1 for axis in range(len(dims))])
    return loudness


def different_ones(own_key, rows, amount, top, lift):
    ranking = jax.random.permutation(jax.random.fold_in(own_key, 1), amount)
    favour = ranking
    for power in range(3):
        favour = favour * favour // amount
    favour = favour * lift // amount
    lots = jax.random.randint(jax.random.fold_in(own_key, 2), (rows, amount), 0, 4096) + favour
    fixed_rows = jax.random.permutation(jax.random.fold_in(own_key, 3), rows)[jnp.arange(amount) % rows]
    lots = jnp.where(jnp.arange(rows)[:, None] == fixed_rows[None, :], 1 << 14, lots)
    priority = lots * amount + jnp.arange(amount)
    return lax.top_k(priority.astype(jnp.int32), top)[1].astype(jnp.int32)


def gaussian(key, shape, width, most, cuts=(), kind=jnp.bfloat16):
    factor_of = shard_levels(key, shape, cuts, -0.22, 0.18) if cuts else 1.0
    entries = jax.random.normal(key, shape, jnp.float32) * width * factor_of
    return jnp.minimum(jnp.maximum(entries, -most), most).astype(kind)


def setup_inputs(seed: int = 0) -> dict:
    seeds = jax.random.split(jax.random.key(seed), 15)
    return {
        "tokens": gaussian(seeds[0], (TOKENS, MODEL_WIDTH), 1.0, 6.0, ((0, 8), (1, 4))),
        "owners": jax.random.permutation(seeds[1], N_REQ).astype(jnp.int32),
        "request_groups": different_ones(seeds[2], N_REQ, GROUPS, 2, 4096),
        "request_lengths": draw_request_lengths(jax.random.fold_in(seeds[14], 71), 0),
        "prefix_cache": draw_prefix_cache(jax.random.fold_in(seeds[14], 71), 0),
        "attn_gain": jnp.clip(1.0 + 0.1 * jax.random.normal(seeds[5], (MODEL_WIDTH,), jnp.float32), 0.5, 1.5),
        "query_weight": gaussian(seeds[6], (MODEL_WIDTH, HQ * HEAD_SIZE), MODEL_WIDTH ** -0.5, 0.125, ((1, 4),)),
        "key_value_weight": gaussian(seeds[7], (MODEL_WIDTH, 2 * KEY_VALUE_HEADS * HEAD_SIZE), MODEL_WIDTH ** -0.5, 0.125),
        "query_gain": draw_query_gain(jax.random.fold_in(seeds[14], 71), 0),
        "key_gain": draw_key_gain(jax.random.fold_in(seeds[14], 71), 0),
        "w_out": gaussian(seeds[10], (HQ * HEAD_SIZE, MODEL_WIDTH), (HQ * HEAD_SIZE) ** -0.5, 0.15625, ((0, 4),)),
        "ffn_gain": jnp.clip(1.0 + 0.1 * jax.random.normal(seeds[11], (MODEL_WIDTH,), jnp.float32), 0.5, 1.5),
        "w_gate_up": gaussian(seeds[12], (MODEL_WIDTH, 2, FF), MODEL_WIDTH ** -0.5, 0.125, ((2, 4),)),
        "w_down": gaussian(seeds[13], (FF, MODEL_WIDTH), FF ** -0.5, 0.078125, ((0, 4),)),
    }


eps_norm = 1e-06
rope_base = 10000.0
masked_score = -1e+30

def to_bf16(array_in):
    return lax.optimization_barrier(array_in.astype(jnp.bfloat16))

def rms_scale(values, gain_vec):
    mean_sq = lax.optimization_barrier(jnp.mean(values * values, axis=-1, keepdims=True))
    return values * lax.rsqrt(mean_sq + eps_norm) * gain_vec

def rotate(values, positions):
    half_size = values.shape[-1] // 2
    frequency = rope_base ** (-jnp.arange(half_size, dtype=jnp.float32) * 2.0 / values.shape[-1])
    angles = positions.astype(jnp.float32)[:, None] * frequency[None, :]
    cos_part = jnp.cos(angles)[:, None, :]
    sin_part = jnp.sin(angles)[:, None, :]
    front_half = values[..., :half_size]
    back_half = values[..., half_size:]
    return jnp.concatenate([front_half * cos_part - back_half * sin_part, back_half * cos_part + front_half * sin_part], axis=-1)

def partial_attend(query_rows, key_rows, value_rows, allowed):
    score_scale = query_rows.shape[-1] ** (-0.5)
    scores = jnp.einsum('rhd,shd->hrs', query_rows.astype(jnp.float32), key_rows.astype(jnp.float32)) * score_scale
    if allowed is not None:
        scores = jnp.where(allowed[None], scores, masked_score)
    row_max = lax.optimization_barrier(jnp.max(scores, axis=-1, keepdims=True))
    weights = jnp.exp(scores - row_max)
    row_total = lax.optimization_barrier(jnp.sum(weights, axis=-1, keepdims=True))
    blended = jnp.einsum('hrs,shd->rhd', to_bf16(weights).astype(jnp.float32), value_rows.astype(jnp.float32))
    blended = blended / jnp.transpose(row_total, (1, 0, 2))
    log_total = jnp.transpose(row_max + jnp.log(row_total), (1, 0, 2))[..., 0]
    return (blended, log_total)

def combine(out_parts, lse_parts):
    row_max = jnp.maximum(jnp.maximum(lse_parts[0], lse_parts[1]), lse_parts[2])
    factors = [jnp.exp(log_part - row_max) for log_part in lse_parts]
    row_total = factors[0] + factors[1] + factors[2]
    blended = factors[0][..., None] * out_parts[0].astype(jnp.float32)
    blended = blended + factors[1][..., None] * out_parts[1].astype(jnp.float32)
    blended = blended + factors[2][..., None] * out_parts[2].astype(jnp.float32)
    return blended / row_total[..., None]

def reference(tokens, owners, request_groups, request_lengths, prefix_cache, attn_gain, query_weight, key_value_weight, query_gain, key_gain, w_out, ffn_gain, w_gate_up, w_down):
    key_value_columns = KEY_VALUE_HEADS * HEAD_SIZE
    out_weight = w_out.astype(jnp.float32).reshape(N_TP, key_value_columns, MODEL_WIDTH)
    down_weight = w_down.astype(jnp.float32).reshape(N_TP, FF // N_TP, MODEL_WIDTH)

    def one_block(block_args):
        rows_in, group_ids, lengths = block_args
        row_index = jnp.arange(SUFFIX_TOKENS, dtype=jnp.int32)
        first_len = lengths[0].astype(jnp.int32)
        segment = (row_index >= first_len).astype(jnp.int32)
        position = row_index - segment * first_len + PREFIX
        residual_in = rows_in.astype(jnp.float32)
        normalized_input = to_bf16(rms_scale(residual_in, attn_gain))
        query_rows = jnp.dot(normalized_input, query_weight, preferred_element_type=jnp.float32).reshape(SUFFIX_TOKENS, N_TP * KEY_VALUE_HEADS, HEAD_SIZE)
        query_rows = to_bf16(rotate(rms_scale(query_rows, query_gain), position))
        key_value_rows = jnp.dot(normalized_input, key_value_weight, preferred_element_type=jnp.float32).reshape(SUFFIX_TOKENS, 2, KEY_VALUE_HEADS, HEAD_SIZE)
        key_rows = to_bf16(rotate(rms_scale(key_value_rows[:, 0], key_gain), position))
        value_rows = to_bf16(key_value_rows[:, 1])
        cache_rows = jnp.stack([key_rows.reshape(SUFFIX_TOKENS, key_value_columns), value_rows.reshape(SUFFIX_TOKENS, key_value_columns)], axis=1)
        allowed = (segment[:, None] == segment[None, :]) & (row_index[None, :] <= row_index[:, None])
        own_out, own_lse = partial_attend(query_rows, jnp.tile(key_rows, (1, N_TP, 1)), jnp.tile(value_rows, (1, N_TP, 1)), allowed)
        half_outs = []
        half_lses = []
        for half_index in range(2):
            picked_out = []
            picked_lse = []
            for request in range(2):
                holder = owners[2 * group_ids[request] + half_index].astype(jnp.int32)
                stored_slot = lax.dynamic_index_in_dim(prefix_cache, holder, 0, keepdims=False)
                stored_keys = jnp.tile(stored_slot[0].reshape(PREFIX_HALF_LEN, KEY_VALUE_HEADS, HEAD_SIZE), (1, N_TP, 1))
                stored_values = jnp.tile(stored_slot[1].reshape(PREFIX_HALF_LEN, KEY_VALUE_HEADS, HEAD_SIZE), (1, N_TP, 1))
                blended, log_total = partial_attend(query_rows, stored_keys, stored_values, None)
                picked_out.append(to_bf16(blended))
                picked_lse.append(log_total)
            first_rows = segment == 0
            half_outs.append(jnp.where(first_rows[:, None, None], picked_out[0], picked_out[1]))
            half_lses.append(jnp.where(first_rows[:, None], picked_lse[0], picked_lse[1]))
        attention = to_bf16(combine([half_outs[0], half_outs[1], own_out], [half_lses[0], half_lses[1], own_lse]))
        attention = attention.reshape(SUFFIX_TOKENS, N_TP, key_value_columns).astype(jnp.float32)
        head_parts = to_bf16(jnp.einsum('rtc,tcd->rtd', attention, out_weight)).astype(jnp.float32)
        mixed = residual_in + lax.optimization_barrier(jnp.sum(head_parts, axis=1))
        normed_ffn = to_bf16(rms_scale(mixed, ffn_gain))
        gate_part = jnp.dot(normed_ffn, w_gate_up[:, 0], preferred_element_type=jnp.float32)
        up_part = jnp.dot(normed_ffn, w_gate_up[:, 1], preferred_element_type=jnp.float32)
        activated = to_bf16(jax.nn.silu(gate_part) * up_part).reshape(SUFFIX_TOKENS, N_TP, FF // N_TP).astype(jnp.float32)
        down_parts = to_bf16(jnp.einsum('rtf,tfd->rtd', activated, down_weight)).astype(jnp.float32)
        hidden_rows = (mixed + lax.optimization_barrier(jnp.sum(down_parts, axis=1))).astype(jnp.bfloat16)
        return (hidden_rows, cache_rows)
    hidden_all, cache_all = lax.map(one_block, (tokens.reshape(N_REQ, SUFFIX_TOKENS, MODEL_WIDTH), request_groups, request_lengths))
    return (hidden_all.reshape(TOKENS, MODEL_WIDTH), cache_all.reshape(TOKENS, 2, key_value_columns))
```

```python
import functools

import jax
import jax.numpy as jnp
from jax import lax
from jax.experimental import pallas as pl
from jax.experimental.pallas import tpu as pltpu
from jax.sharding import PartitionSpec as P

HEAD_SIZE = 64
PREFIX = 1536

eps_norm = 1e-06
rope_base = 10000.0
masked_score = -1e30
VMEM_LIMIT = 60 * 1024 * 1024


def rms_scale(values, gain_vec):
    mean_sq = jnp.mean(values * values, axis=-1, keepdims=True)
    return values * lax.rsqrt(mean_sq + eps_norm) * gain_vec


def rotate(values, positions):
    half_size = values.shape[-1] // 2
    frequency = rope_base ** (-jnp.arange(half_size, dtype=jnp.float32) * 2.0 / values.shape[-1])
    angles = positions.astype(jnp.float32)[:, None] * frequency[None, :]
    cos_part = jnp.cos(angles)[:, None, :]
    sin_part = jnp.sin(angles)[:, None, :]
    front_half = values[..., :half_size]
    back_half = values[..., half_size:]
    return jnp.concatenate(
        [
            front_half * cos_part - back_half * sin_part,
            back_half * cos_part + front_half * sin_part,
        ],
        axis=-1,
    )


def tn_dot(lhs, rhs):
    return lax.dot_general(lhs, rhs, (((0,), (0,)), ((), ())), preferred_element_type=jnp.float32)


def nn_dot(lhs, rhs):
    return lax.dot_general(lhs, rhs, (((1,), (0,)), ((), ())), preferred_element_type=jnp.float32)


def norm_kernel(rank_ref, own_ref, core_ref, chip_ref, both_ref, gain_ref, full_ref, normed_ref):
    rank = rank_ref[0]
    width = own_ref.shape[1]
    pieces = [own_ref, core_ref, chip_ref, both_ref]
    values = [piece[...].astype(jnp.float32) for piece in pieces]
    total = sum(jnp.sum(v * v, axis=-1, keepdims=True) for v in values)
    scale = lax.rsqrt(total / full_ref.shape[1] + eps_norm)
    for flip, (piece, value) in enumerate(zip(pieces, values)):
        place = pl.multiple_of((rank ^ flip) * width, width)
        columns = pl.ds(place, width)
        full_ref[:, columns] = piece[...]
        normed_ref[:, columns] = (value * scale * gain_ref[:, columns]).astype(jnp.bfloat16)


def gather_norm(rank, pieces, gain):
    rows, width = pieces[0].shape
    block = 128
    full = width * len(pieces)
    piece_spec = pl.BlockSpec((block, width), lambda i, s: (i, 0))
    full_spec = pl.BlockSpec((block, full), lambda i, s: (i, 0))
    return pl.pallas_call(
        norm_kernel,
        out_shape=(
            jax.ShapeDtypeStruct((rows, full), jnp.bfloat16),
            jax.ShapeDtypeStruct((rows, full), jnp.bfloat16),
        ),
        grid_spec=pltpu.PrefetchScalarGridSpec(
            num_scalar_prefetch=1,
            grid=(rows // block,),
            in_specs=[piece_spec] * 4 + [pl.BlockSpec((1, full), lambda i, s: (0, 0))],
            out_specs=[full_spec, full_spec],
        ),
        name="gather_norm",
    )(rank.reshape(1), *pieces, gain.reshape(1, full))


def suffix_kernel(len_ref, q_ref, k_ref, v_ref, out_ref, lse_ref):
    first_len = len_ref[0]
    rows = q_ref.shape[1]
    block = 256
    heads = q_ref.shape[0] // HEAD_SIZE
    for start in range(0, rows, block):
        keys = start + block
        key_index = lax.broadcasted_iota(jnp.int32, (keys, block), 0)
        row_index = lax.broadcasted_iota(jnp.int32, (keys, block), 1) + start
        begin = jnp.where(row_index >= first_len, first_len, 0)
        allowed = (key_index <= row_index) & (key_index >= begin)
        for head in range(heads):
            band = pl.ds(head * HEAD_SIZE, HEAD_SIZE)
            scores = tn_dot(k_ref[band, :keys], q_ref[band, start : start + block]) * 0.125
            scores = jnp.where(allowed, scores, masked_score)
            row_max = jnp.max(scores, axis=0, keepdims=True)
            weights = jnp.exp(scores - row_max)
            total = jnp.sum(weights, axis=0, keepdims=True)
            blended = nn_dot(v_ref[band, :keys], weights.astype(jnp.bfloat16))
            out_ref[band, start : start + block] = blended / total
            lse_ref[head : head + 1, start : start + block] = row_max + jnp.log(total)


def suffix_attend(first_len, q_t, k_t, v_t):
    columns, rows = q_t.shape
    vmem = pl.BlockSpec(memory_space=pltpu.VMEM)
    return pl.pallas_call(
        suffix_kernel,
        out_shape=(
            jax.ShapeDtypeStruct((columns, rows), jnp.float32),
            jax.ShapeDtypeStruct((8, rows), jnp.float32),
        ),
        in_specs=[pl.BlockSpec(memory_space=pltpu.SMEM), vmem, vmem, vmem],
        out_specs=[vmem, vmem],
        cost_estimate=pl.CostEstimate(flops=4 * columns * rows * rows, bytes_accessed=3 << 20, transcendentals=5 * rows * rows),
        name="suffix_attend",
    )(first_len.reshape(1), q_t, k_t, v_t)


def prefix_kernel(n_units, meta_ref, own_q_ref, other_q_ref, *refs):
    units = refs[:n_units]
    own_out, own_lse, other_out, other_lse, buffer, sems = refs[n_units:]
    first_len = meta_ref[4]
    heads = own_q_ref.shape[0] // HEAD_SIZE
    block = 256
    blocks = own_q_ref.shape[1] // block
    for job in range(4):
        for unit in range(n_units):

            @pl.when(meta_ref[job] == unit)
            def _():
                pltpu.make_async_copy(units[unit], buffer.at[job], sems.at[job]).start()

    for request in range(2):
        for half in range(2):
            job = 2 * request + half
            pltpu.make_async_copy(units[0], buffer.at[job], sems.at[job]).wait()
        for part in range(blocks):
            start = part * block
            if request == 0:
                present = start < first_len
            else:
                present = start + block > first_len

            @pl.when(present)
            def _():
                lane = lax.broadcasted_iota(jnp.int32, (1, block), 1) + start
                mine = (lane < first_len) if request == 0 else (lane >= first_len)
                cols = pl.ds(start, block)

                for q_ref, out_ref, lse_ref in (
                    (own_q_ref, own_out, own_lse),
                    (other_q_ref, other_out, other_lse),
                ):

                    def one_head(head, carry, q_ref=q_ref, out_ref=out_ref, lse_ref=lse_ref):
                        band = pl.ds(pl.multiple_of(head * HEAD_SIZE, HEAD_SIZE), HEAD_SIZE)
                        query = q_ref[band, cols]
                        scores = [
                            tn_dot(buffer[2 * request + half, 0, band, :], query) * 0.125
                            for half in range(2)
                        ]
                        row_max = jnp.maximum(
                            jnp.max(scores[0], axis=0, keepdims=True),
                            jnp.max(scores[1], axis=0, keepdims=True),
                        )
                        weights = [jnp.exp(s - row_max) for s in scores]
                        total = jnp.sum(weights[0], axis=0, keepdims=True) + jnp.sum(
                            weights[1], axis=0, keepdims=True
                        )
                        blended = sum(
                            nn_dot(buffer[2 * request + half, 1, band, :], weights[half].astype(jnp.bfloat16))
                            for half in range(2)
                        )
                        out = (blended / total).astype(out_ref.dtype)
                        lse = row_max + jnp.log(total)
                        row = pl.ds(head, 1)
                        if request == 1:
                            out = jnp.where(mine, out, out_ref[band, cols])
                            lse = jnp.where(mine, lse, lse_ref[row, cols])
                        out_ref[band, cols] = out
                        lse_ref[row, cols] = lse
                        return carry

                    lax.fori_loop(0, heads, one_head, 0)


def prefix_attend(meta, own_q, other_q, units):
    columns, rows = own_q.shape
    vmem = pl.BlockSpec(memory_space=pltpu.VMEM)
    out = jax.ShapeDtypeStruct((columns, rows), jnp.float32)
    lse = jax.ShapeDtypeStruct((8, rows), jnp.float32)
    sent = jax.ShapeDtypeStruct((columns, rows), jnp.bfloat16)
    return pl.pallas_call(
        functools.partial(prefix_kernel, len(units)),
        out_shape=(out, lse, sent, lse),
        in_specs=[pl.BlockSpec(memory_space=pltpu.SMEM), vmem, vmem]
        + [pl.BlockSpec(memory_space=pl.ANY)] * len(units),
        out_specs=[vmem] * 4,
        scratch_shapes=[
            pltpu.VMEM((4,) + units[0].shape, jnp.bfloat16),
            pltpu.SemaphoreType.DMA((4,)),
        ],
        cost_estimate=pl.CostEstimate(flops=8 * columns * rows * 1536, bytes_accessed=6 << 20, transcendentals=10 * rows * 768),
        name="prefix_attend",
    )(meta, own_q, other_q, *units)


def local(
    n_req,
    tokens,
    owners,
    request_groups,
    request_lengths,
    prefix_cache,
    attn_gain,
    query_weight,
    key_value_weight,
    query_gain,
    key_gain,
    w_out,
    ffn_gain,
    w_gate_up,
    w_down,
):
    row_count, width = tokens.shape
    columns = query_weight.shape[1]
    head_count = columns // HEAD_SIZE
    rank = lax.axis_index("tp")
    my_req = lax.axis_index("req")
    core = rank % 2

    def across_chip(value):
        return lax.ppermute(value, "tp", [(i, i ^ 2) for i in range(4)])

    def across_core(value):
        return lax.ppermute(value, "tp", [(i, i ^ 1) for i in range(4)])

    length = n_req // 2
    share = prefix_cache.shape[2] // 2
    mine = lax.dynamic_slice_in_dim(jnp.transpose(prefix_cache[0], (0, 2, 1)), core * share, share, 2)

    def along(value, sources, step):
        pairs = [(2 * a + b, 2 * (a + step) + b) for a in sources for b in range(2)]
        return lax.ppermute(value, "req", pairs)

    def aside(value, members):
        return lax.ppermute(value, "req", [(2 * a + b, 2 * a + 1 - b) for a in members for b in range(2)])

    below, above = [mine], [mine]
    units = [mine, aside(mine, range(length))]
    for step in range(1, length):
        below.append(along(below[-1], range(step - 1, length - 1), 1))
        above.append(along(above[-1], range(1, length - step + 1), -1))
        units += [
            below[-1],
            aside(below[-1], range(step, length)),
            above[-1],
            aside(above[-1], range(0, length - step)),
        ]
    wanted = owners.reshape(-1, 2)[request_groups[0]].reshape(-1)
    distance = wanted // 2 - my_req // 2
    other_side = (wanted % 2 != my_req % 2).astype(jnp.int32)
    unit_index = jnp.where(
        distance == 0,
        0,
        jnp.where(distance < 0, -4 * distance - 2, 4 * distance),
    ) + other_side

    from_chip = across_chip(tokens)
    from_core = across_core(tokens)
    from_both = across_core(from_chip)
    full_rows, normalized_input = gather_norm(rank, (tokens, from_core, from_chip, from_both), attn_gain)

    w_out_held, _ = lax.optimization_barrier((w_out, from_chip))
    w_out_chip = across_chip(w_out_held)
    w_out_core = across_core(w_out_held)
    w_out_both = across_core(w_out_chip)
    w_out_all = jnp.concatenate([w_out, w_out_core, w_out_chip, w_out_both], axis=0)

    row_index = jnp.arange(row_count, dtype=jnp.int32)
    first_len = request_lengths[0, 0]
    segment = (row_index >= first_len).astype(jnp.int32)
    position = row_index - segment * first_len + PREFIX
    query_rows = jnp.dot(
        normalized_input, query_weight, preferred_element_type=jnp.float32
    ).reshape(row_count, head_count, HEAD_SIZE)
    query_rows = rotate(rms_scale(query_rows, query_gain), position).astype(jnp.bfloat16)
    key_value_rows = jnp.dot(
        normalized_input, key_value_weight, preferred_element_type=jnp.float32
    ).reshape(row_count, 2, head_count, HEAD_SIZE)
    key_rows = rotate(rms_scale(key_value_rows[:, 0], key_gain), position).astype(jnp.bfloat16)
    value_rows = key_value_rows[:, 1].astype(jnp.bfloat16)
    cache_rows = jnp.stack(
        [key_rows.reshape(row_count, columns), value_rows.reshape(row_count, columns)],
        axis=1,
    )
    own_q = query_rows.reshape(row_count, columns).T
    other_q = across_core(own_q)
    suffix_out, suffix_lse = suffix_attend(
        first_len, own_q, key_rows.reshape(row_count, columns).T, value_rows.reshape(row_count, columns).T
    )

    meta = jnp.concatenate([unit_index.astype(jnp.int32), first_len.reshape(1)])
    own_out, own_lse, sent_out, sent_lse = prefix_attend(meta, own_q, other_q, units)
    got_out = across_core(sent_out)
    got_lse = across_core(sent_lse)

    outs = [
        part.astype(jnp.float32).reshape(head_count, HEAD_SIZE, row_count)
        for part in (own_out, got_out, suffix_out)
    ]
    lses = [part[:head_count, None, :] for part in (own_lse, got_lse, suffix_lse)]
    top = jnp.maximum(jnp.maximum(lses[0], lses[1]), lses[2])
    factors = [jnp.exp(part - top) for part in lses]
    blended = sum(f * o for f, o in zip(factors, outs))
    attention = (blended / (factors[0] + factors[1] + factors[2])).astype(jnp.bfloat16)
    attention = attention.reshape(columns, row_count)

    att_chip = across_chip(attention)
    att_core = across_core(attention)
    att_both = across_core(att_chip)
    att_all = jnp.concatenate([attention, att_core, att_chip, att_both], axis=0)
    head_total = tn_dot(att_all, w_out_all)
    mixed = full_rows.astype(jnp.float32) + head_total

    normed_ffn = rms_scale(mixed, ffn_gain).astype(jnp.bfloat16)
    gate_up = jnp.einsum("rd,dgf->rgf", normed_ffn, w_gate_up, preferred_element_type=jnp.float32)
    activated = (jax.nn.silu(gate_up[:, 0]) * gate_up[:, 1]).astype(jnp.bfloat16)
    down_part = jnp.dot(activated, w_down, preferred_element_type=jnp.float32).astype(jnp.bfloat16)

    def block_of(value, flip):
        return lax.dynamic_slice_in_dim(value, (rank ^ flip) * width, width, 1)

    got_far = across_core(block_of(down_part, 3))
    got_near = across_core(block_of(down_part, 1))
    far_sum = (block_of(down_part, 2).astype(jnp.float32) + got_far.astype(jnp.float32)).astype(jnp.bfloat16)
    near_sum = block_of(mixed, 0) + block_of(down_part, 0).astype(jnp.float32) + got_near.astype(jnp.float32)
    hidden = near_sum + across_chip(far_sum).astype(jnp.float32)
    return (hidden.astype(jnp.bfloat16), cache_rows)


def solution(mesh):
    placed = (
        P("req", "tp"),
        P(),
        P("req", None),
        P("req", None),
        P("req", None, None, None),
        P(),
        P(None, "tp"),
        P(),
        P(),
        P(),
        P("tp", None),
        P(),
        P(None, None, "tp"),
        P("tp", None),
    )
    return jax.shard_map(
        functools.partial(local, mesh.shape["req"]),
        mesh=mesh,
        in_specs=placed,
        out_specs=(P("req", "tp"), P("req", None, None)),
        check_vma=False,
    )
```

```python
import functools

import jax
import jax.numpy as jnp
from jax import lax
from jax.experimental import pallas as pl
from jax.experimental.pallas import tpu as pltpu
from jax.sharding import PartitionSpec as P

HEAD_SIZE = 64
PREFIX = 1536

eps_norm = 1e-06
rope_base = 10000.0
masked_score = -1e30
VMEM_LIMIT = 60 * 1024 * 1024


def rms_scale(values, gain_vec):
    mean_sq = jnp.mean(values * values, axis=-1, keepdims=True)
    return values * lax.rsqrt(mean_sq + eps_norm) * gain_vec


def rotate(values, positions):
    half_size = values.shape[-1] // 2
    frequency = rope_base ** (-jnp.arange(half_size, dtype=jnp.float32) * 2.0 / values.shape[-1])
    angles = positions.astype(jnp.float32)[:, None] * frequency[None, :]
    cos_part = jnp.cos(angles)[:, None, :]
    sin_part = jnp.sin(angles)[:, None, :]
    front_half = values[..., :half_size]
    back_half = values[..., half_size:]
    return jnp.concatenate(
        [
            front_half * cos_part - back_half * sin_part,
            back_half * cos_part + front_half * sin_part,
        ],
        axis=-1,
    )


def tn_dot(lhs, rhs):
    return lax.dot_general(lhs, rhs, (((0,), (0,)), ((), ())), preferred_element_type=jnp.float32)


def nn_dot(lhs, rhs):
    return lax.dot_general(lhs, rhs, (((1,), (0,)), ((), ())), preferred_element_type=jnp.float32)


def norm_kernel(rank_ref, own_ref, core_ref, chip_ref, both_ref, gain_ref, full_ref, normed_ref):
    rank = rank_ref[0]
    width = own_ref.shape[1]
    pieces = [own_ref, core_ref, chip_ref, both_ref]
    values = [piece[...].astype(jnp.float32) for piece in pieces]
    total = sum(jnp.sum(v * v, axis=-1, keepdims=True) for v in values)
    scale = lax.rsqrt(total / full_ref.shape[1] + eps_norm)
    for flip, (piece, value) in enumerate(zip(pieces, values)):
        place = pl.multiple_of((rank ^ flip) * width, width)
        columns = pl.ds(place, width)
        full_ref[:, columns] = piece[...]
        normed_ref[:, columns] = (value * scale * gain_ref[:, columns]).astype(jnp.bfloat16)


def gather_norm(rank, pieces, gain):
    rows, width = pieces[0].shape
    block = 128
    full = width * len(pieces)
    piece_spec = pl.BlockSpec((block, width), lambda i, s: (i, 0))
    full_spec = pl.BlockSpec((block, full), lambda i, s: (i, 0))
    return pl.pallas_call(
        norm_kernel,
        out_shape=(
            jax.ShapeDtypeStruct((rows, full), jnp.bfloat16),
            jax.ShapeDtypeStruct((rows, full), jnp.bfloat16),
        ),
        grid_spec=pltpu.PrefetchScalarGridSpec(
            num_scalar_prefetch=1,
            grid=(rows // block,),
            in_specs=[piece_spec] * 4 + [pl.BlockSpec((1, full), lambda i, s: (0, 0))],
            out_specs=[full_spec, full_spec],
        ),
        name="gather_norm",
    )(rank.reshape(1), *pieces, gain.reshape(1, full))


def suffix_kernel(len_ref, q_ref, k_ref, v_ref, out_ref, lse_ref):
    first_len = len_ref[0]
    rows = q_ref.shape[1]
    block = 256
    heads = q_ref.shape[0] // HEAD_SIZE
    for start in range(0, rows, block):
        keys = start + block
        key_index = lax.broadcasted_iota(jnp.int32, (keys, block), 0)
        row_index = lax.broadcasted_iota(jnp.int32, (keys, block), 1) + start
        begin = jnp.where(row_index >= first_len, first_len, 0)
        allowed = (key_index <= row_index) & (key_index >= begin)
        for head in range(heads):
            band = pl.ds(head * HEAD_SIZE, HEAD_SIZE)
            scores = tn_dot(k_ref[band, :keys], q_ref[band, start : start + block])
            scores = jnp.where(allowed, scores, masked_score)
            row_max = jnp.max(scores, axis=0, keepdims=True)
            weights = jnp.exp(scores - row_max)
            total = jnp.sum(weights, axis=0, keepdims=True)
            blended = nn_dot(v_ref[band, :keys], weights.astype(jnp.bfloat16))
            out_ref[band, start : start + block] = blended / total
            lse_ref[head : head + 1, start : start + block] = row_max + jnp.log(total)


def suffix_attend(first_len, q_t, k_t, v_t):
    columns, rows = q_t.shape
    vmem = pl.BlockSpec(memory_space=pltpu.VMEM)
    return pl.pallas_call(
        suffix_kernel,
        out_shape=(
            jax.ShapeDtypeStruct((columns, rows), jnp.float32),
            jax.ShapeDtypeStruct((8, rows), jnp.float32),
        ),
        in_specs=[pl.BlockSpec(memory_space=pltpu.SMEM), vmem, vmem, vmem],
        out_specs=[vmem, vmem],
        cost_estimate=pl.CostEstimate(flops=4 * columns * rows * rows, bytes_accessed=3 << 20, transcendentals=5 * rows * rows),
        name="suffix_attend",
    )(first_len.reshape(1), q_t, k_t, v_t)


def fold(values, op):
    return op(values.reshape(values.shape[0] // 8, 8, values.shape[1]), axis=0)


def prefix_kernel(block, chunk, n_units, meta_ref, own_q_ref, other_q_ref, *refs):
    units = refs[:n_units]
    (own_out, own_lse, other_out, other_lse), scratch = refs[n_units : n_units + 4], refs[n_units + 4 :]
    kv, q_buf, o_buf, l_buf, s_a, s_b, m_a, m_b, sems = scratch
    first_len = meta_ref[4]
    share = units[0].shape[2]

    def landing(job):
        return kv.at[job // 2, :, :, pl.ds((job % 2) * share, share)]

    for job in range(4):
        for unit in range(n_units):

            @pl.when(meta_ref[job] == unit)
            def _():
                pltpu.make_async_copy(units[unit], landing(job), sems.at[job]).start()

    columns, rows = own_q_ref.shape
    q_buf[:columns] = own_q_ref[...]
    q_buf[columns:] = other_q_ref[...]
    for job in range(4):
        pltpu.make_async_copy(units[0], landing(job), sems.at[job]).wait()

    heads = columns // HEAD_SIZE
    per = 2 * heads
    keys = 2 * share
    n_first = (first_len + block - 1) // block
    skipped = first_len // block
    pairs = n_first + rows // block - skipped

    def place(task):
        pair = task // per
        head = task % per
        second = (pair >= n_first).astype(jnp.int32)
        part = jnp.where(second == 1, pair - n_first + skipped, pair)
        cols = pl.ds(pl.multiple_of(part * block, block), block)
        q_band = pl.ds(pl.multiple_of(head * HEAD_SIZE, HEAD_SIZE), HEAD_SIZE)
        k_band = pl.ds(pl.multiple_of((head % heads) * HEAD_SIZE, HEAD_SIZE), HEAD_SIZE)
        return second, part, cols, q_band, k_band, head

    def step(now, later, s_now, m_now, s_later, m_later):
        if now is not None:
            second, part, cols, q_band, k_band, head = place(now)
            peak = m_now[...]
        later_second, _, later_cols, later_q, later_k, _ = place(later)
        query = q_buf[later_q, later_cols]
        top = total = blended = None
        for start in range(0, keys, chunk):
            span = pl.ds(start, chunk)
            scores = tn_dot(kv[later_second, 0, later_k, span], query)
            s_later[span, :] = scores
            folded = fold(scores, jnp.max)
            top = folded if top is None else jnp.maximum(top, folded)
            if now is not None:
                weights = jnp.exp(s_now[span, :] - peak)
                folded = fold(weights, jnp.sum)
                total = folded if total is None else total + folded
                out = nn_dot(kv[second, 1, k_band, span], weights.astype(jnp.bfloat16))
                blended = out if blended is None else blended + out
        m_later[...] = jnp.max(top, axis=0, keepdims=True)
        if now is not None:
            total = jnp.sum(total, axis=0, keepdims=True)
            lane = lax.broadcasted_iota(jnp.int32, (1, block), 1) + part * block
            mine = (lane >= first_len).astype(jnp.int32) == second
            o_buf[q_band, cols] = jnp.where(mine, blended * (1.0 / total), o_buf[q_band, cols])
            row = pl.ds(head, 1)
            l_buf[row, cols] = jnp.where(mine, peak + jnp.log(total), l_buf[row, cols])

    step(None, 0, None, None, s_a, m_a)

    def two(index, carry):
        task = 2 * index
        step(task, task + 1, s_a, m_a, s_b, m_b)
        step(task + 1, jnp.minimum(task + 2, pairs * per - 1), s_b, m_b, s_a, m_a)
        return carry

    lax.fori_loop(0, pairs * heads, two, 0)
    own_out[...] = o_buf[:columns]
    other_out[...] = o_buf[columns:].astype(jnp.bfloat16)
    own_lse[:heads] = l_buf[:heads]
    other_lse[:heads] = l_buf[heads:per]


def prefix_attend(meta, own_q, other_q, units):
    columns, rows = own_q.shape
    share = units[0].shape[2]
    block = 256
    vmem = pl.BlockSpec(memory_space=pltpu.VMEM)
    out = jax.ShapeDtypeStruct((columns, rows), jnp.float32)
    lse = jax.ShapeDtypeStruct((8, rows), jnp.float32)
    sent = jax.ShapeDtypeStruct((columns, rows), jnp.bfloat16)
    return pl.pallas_call(
        functools.partial(prefix_kernel, block, 256, len(units)),
        out_shape=(out, lse, sent, lse),
        in_specs=[pl.BlockSpec(memory_space=pltpu.SMEM), vmem, vmem]
        + [pl.BlockSpec(memory_space=pl.ANY)] * len(units),
        out_specs=[vmem] * 4,
        scratch_shapes=[
            pltpu.VMEM((2, 2, columns, 2 * share), jnp.bfloat16),
            pltpu.VMEM((2 * columns, rows), jnp.bfloat16),
            pltpu.VMEM((2 * columns, rows), jnp.float32),
            pltpu.VMEM((16, rows), jnp.float32),
            pltpu.VMEM((2 * share, block), jnp.float32),
            pltpu.VMEM((2 * share, block), jnp.float32),
            pltpu.VMEM((1, block), jnp.float32),
            pltpu.VMEM((1, block), jnp.float32),
            pltpu.SemaphoreType.DMA((4,)),
        ],
        cost_estimate=pl.CostEstimate(
            flops=16 * columns * rows * share, bytes_accessed=6 << 20, transcendentals=20 * rows * share
        ),
        name="prefix_attend",
    )(meta, own_q, other_q, *units)


def local(
    n_req,
    tokens,
    owners,
    request_groups,
    request_lengths,
    prefix_cache,
    attn_gain,
    query_weight,
    key_value_weight,
    query_gain,
    key_gain,
    w_out,
    ffn_gain,
    w_gate_up,
    w_down,
):
    row_count, width = tokens.shape
    columns = query_weight.shape[1]
    head_count = columns // HEAD_SIZE
    rank = lax.axis_index("tp")
    my_req = lax.axis_index("req")
    core = rank % 2

    def across_chip(value):
        return lax.ppermute(value, "tp", [(i, i ^ 2) for i in range(4)])

    def across_core(value):
        return lax.ppermute(value, "tp", [(i, i ^ 1) for i in range(4)])

    length = n_req // 2
    share = prefix_cache.shape[2] // 2
    mine = lax.dynamic_slice_in_dim(jnp.transpose(prefix_cache[0], (0, 2, 1)), core * share, share, 2)

    def ring(value):
        return lax.ppermute(value, "req", [(r, (r + 2) % n_req) for r in range(n_req)])

    def aside(value):
        return lax.ppermute(value, "req", [(r, r ^ 1) for r in range(n_req)])

    held = [mine]
    for _ in range(length - 1):
        held.append(ring(held[-1]))
    units = [part for unit in held for part in (unit, aside(unit))]
    wanted = owners.reshape(-1, 2)[request_groups[0]].reshape(-1)
    distance = (my_req // 2 - wanted // 2) % length
    unit_index = 2 * distance + (wanted % 2 != my_req % 2).astype(jnp.int32)

    from_chip = across_chip(tokens)
    from_core = across_core(tokens)
    from_both = across_core(from_chip)
    full_rows, normalized_input = gather_norm(rank, (tokens, from_core, from_chip, from_both), attn_gain)

    w_out_held, _ = lax.optimization_barrier((w_out, from_chip))
    w_out_chip = across_chip(w_out_held)
    w_out_core = across_core(w_out_held)
    w_out_both = across_core(w_out_chip)
    w_out_all = jnp.concatenate([w_out, w_out_core, w_out_chip, w_out_both], axis=0)

    row_index = jnp.arange(row_count, dtype=jnp.int32)
    first_len = request_lengths[0, 0]
    segment = (row_index >= first_len).astype(jnp.int32)
    position = row_index - segment * first_len + PREFIX
    query_rows = jnp.dot(
        normalized_input, query_weight, preferred_element_type=jnp.float32
    ).reshape(row_count, head_count, HEAD_SIZE)
    query_rows = rotate(rms_scale(query_rows, query_gain), position).astype(jnp.bfloat16)
    key_value_rows = jnp.dot(
        normalized_input, key_value_weight, preferred_element_type=jnp.float32
    ).reshape(row_count, 2, head_count, HEAD_SIZE)
    key_rows = rotate(rms_scale(key_value_rows[:, 0], key_gain), position).astype(jnp.bfloat16)
    value_rows = key_value_rows[:, 1].astype(jnp.bfloat16)
    cache_rows = jnp.stack(
        [key_rows.reshape(row_count, columns), value_rows.reshape(row_count, columns)],
        axis=1,
    )
    own_q = (query_rows * HEAD_SIZE**-0.5).reshape(row_count, columns).T
    other_q = across_core(own_q)
    suffix_out, suffix_lse = suffix_attend(
        first_len, own_q, key_rows.reshape(row_count, columns).T, value_rows.reshape(row_count, columns).T
    )

    own_q, suffix_out, suffix_lse = lax.optimization_barrier((own_q, suffix_out, suffix_lse))
    meta = jnp.concatenate([unit_index.astype(jnp.int32), first_len.reshape(1)])
    own_out, own_lse, sent_out, sent_lse = prefix_attend(meta, own_q, other_q, units)
    got_out = across_core(sent_out)
    got_lse = across_core(sent_lse)

    outs = [
        part.astype(jnp.float32).reshape(head_count, HEAD_SIZE, row_count)
        for part in (own_out, got_out, suffix_out)
    ]
    lses = [part[:head_count, None, :] for part in (own_lse, got_lse, suffix_lse)]
    top = jnp.maximum(jnp.maximum(lses[0], lses[1]), lses[2])
    factors = [jnp.exp(part - top) for part in lses]
    blended = sum(f * o for f, o in zip(factors, outs))
    attention = (blended / (factors[0] + factors[1] + factors[2])).astype(jnp.bfloat16)
    attention = attention.reshape(columns, row_count)

    att_chip = across_chip(attention)
    att_core = across_core(attention)
    att_both = across_core(att_chip)
    att_all = jnp.concatenate([attention, att_core, att_chip, att_both], axis=0)
    head_total = tn_dot(att_all, w_out_all)
    mixed = full_rows.astype(jnp.float32) + head_total

    normed_ffn = rms_scale(mixed, ffn_gain).astype(jnp.bfloat16)
    gate_up = jnp.einsum("rd,dgf->rgf", normed_ffn, w_gate_up, preferred_element_type=jnp.float32)
    activated = (jax.nn.silu(gate_up[:, 0]) * gate_up[:, 1]).astype(jnp.bfloat16)
    down_part = jnp.dot(activated, w_down, preferred_element_type=jnp.float32).astype(jnp.bfloat16)

    def block_of(value, flip):
        return lax.dynamic_slice_in_dim(value, (rank ^ flip) * width, width, 1)

    got_far = across_core(block_of(down_part, 3))
    got_near = across_core(block_of(down_part, 1))
    far_sum = (block_of(down_part, 2).astype(jnp.float32) + got_far.astype(jnp.float32)).astype(jnp.bfloat16)
    near_sum = block_of(mixed, 0) + block_of(down_part, 0).astype(jnp.float32) + got_near.astype(jnp.float32)
    hidden = near_sum + across_chip(far_sum).astype(jnp.float32)
    return (hidden.astype(jnp.bfloat16), cache_rows)


def solution(mesh):
    placed = (
        P("req", "tp"),
        P(),
        P("req", None),
        P("req", None),
        P("req", None, None, None),
        P(),
        P(None, "tp"),
        P(),
        P(),
        P(),
        P("tp", None),
        P(),
        P(None, None, "tp"),
        P("tp", None),
    )
    return jax.shard_map(
        functools.partial(local, mesh.shape["req"]),
        mesh=mesh,
        in_specs=placed,
        out_specs=(P("req", "tp"), P("req", None, None)),
        check_vma=False,
    )
```

```python
import functools

import jax
import jax.numpy as jnp
from jax import lax
from jax.experimental import pallas as pl
from jax.experimental.pallas import tpu as pltpu
from jax.sharding import PartitionSpec as P

HEAD_SIZE = 64
PREFIX = 1536

eps_norm = 1e-06
rope_base = 10000.0
masked_score = -1e30
VMEM_LIMIT = 60 * 1024 * 1024


def rms_scale(values, gain_vec):
    mean_sq = jnp.mean(values * values, axis=-1, keepdims=True)
    return values * lax.rsqrt(mean_sq + eps_norm) * gain_vec


def rotate(values, positions):
    half_size = values.shape[-1] // 2
    frequency = rope_base ** (-jnp.arange(half_size, dtype=jnp.float32) * 2.0 / values.shape[-1])
    angles = positions.astype(jnp.float32)[:, None] * frequency[None, :]
    cos_part = jnp.cos(angles)[:, None, :]
    sin_part = jnp.sin(angles)[:, None, :]
    front_half = values[..., :half_size]
    back_half = values[..., half_size:]
    return jnp.concatenate(
        [
            front_half * cos_part - back_half * sin_part,
            back_half * cos_part + front_half * sin_part,
        ],
        axis=-1,
    )


def tn_dot(lhs, rhs):
    return lax.dot_general(lhs, rhs, (((0,), (0,)), ((), ())), preferred_element_type=jnp.float32)


def nn_dot(lhs, rhs):
    return lax.dot_general(lhs, rhs, (((1,), (0,)), ((), ())), preferred_element_type=jnp.float32)


def norm_kernel(rank_ref, own_ref, core_ref, chip_ref, both_ref, gain_ref, full_ref, normed_ref):
    rank = rank_ref[0]
    width = own_ref.shape[1]
    pieces = [own_ref, core_ref, chip_ref, both_ref]
    values = [piece[...].astype(jnp.float32) for piece in pieces]
    total = sum(jnp.sum(v * v, axis=-1, keepdims=True) for v in values)
    scale = lax.rsqrt(total / full_ref.shape[1] + eps_norm)
    for flip, (piece, value) in enumerate(zip(pieces, values)):
        place = pl.multiple_of((rank ^ flip) * width, width)
        columns = pl.ds(place, width)
        full_ref[:, columns] = piece[...]
        normed_ref[:, columns] = (value * scale * gain_ref[:, columns]).astype(jnp.bfloat16)


def gather_norm(rank, pieces, gain):
    rows, width = pieces[0].shape
    block = 128
    full = width * len(pieces)
    piece_spec = pl.BlockSpec((block, width), lambda i, s: (i, 0))
    full_spec = pl.BlockSpec((block, full), lambda i, s: (i, 0))
    return pl.pallas_call(
        norm_kernel,
        out_shape=(
            jax.ShapeDtypeStruct((rows, full), jnp.bfloat16),
            jax.ShapeDtypeStruct((rows, full), jnp.bfloat16),
        ),
        grid_spec=pltpu.PrefetchScalarGridSpec(
            num_scalar_prefetch=1,
            grid=(rows // block,),
            in_specs=[piece_spec] * 4 + [pl.BlockSpec((1, full), lambda i, s: (0, 0))],
            out_specs=[full_spec, full_spec],
        ),
        name="gather_norm",
    )(rank.reshape(1), *pieces, gain.reshape(1, full))


def suffix_kernel(len_ref, q_ref, k_ref, v_ref, out_ref, lse_ref):
    first_len = len_ref[0]
    rows = q_ref.shape[1]
    block = 256
    heads = q_ref.shape[0] // HEAD_SIZE
    for start in range(0, rows, block):
        keys = start + block
        key_index = lax.broadcasted_iota(jnp.int32, (keys, block), 0)
        row_index = lax.broadcasted_iota(jnp.int32, (keys, block), 1) + start
        begin = jnp.where(row_index >= first_len, first_len, 0)
        allowed = (key_index <= row_index) & (key_index >= begin)
        for head in range(heads):
            band = pl.ds(head * HEAD_SIZE, HEAD_SIZE)
            scores = tn_dot(k_ref[band, :keys], q_ref[band, start : start + block])
            scores = jnp.where(allowed, scores, masked_score)
            row_max = jnp.max(scores, axis=0, keepdims=True)
            weights = jnp.exp(scores - row_max)
            total = jnp.sum(weights, axis=0, keepdims=True)
            blended = nn_dot(v_ref[band, :keys], weights.astype(jnp.bfloat16))
            out_ref[band, start : start + block] = blended / total
            lse_ref[head : head + 1, start : start + block] = row_max + jnp.log(total)


def suffix_attend(first_len, q_t, k_t, v_t):
    columns, rows = q_t.shape
    vmem = pl.BlockSpec(memory_space=pltpu.VMEM)
    return pl.pallas_call(
        suffix_kernel,
        out_shape=(
            jax.ShapeDtypeStruct((columns, rows), jnp.float32),
            jax.ShapeDtypeStruct((8, rows), jnp.float32),
        ),
        in_specs=[pl.BlockSpec(memory_space=pltpu.SMEM), vmem, vmem, vmem],
        out_specs=[vmem, vmem],
        cost_estimate=pl.CostEstimate(flops=4 * columns * rows * rows, bytes_accessed=3 << 20, transcendentals=5 * rows * rows),
        name="suffix_attend",
    )(first_len.reshape(1), q_t, k_t, v_t)


def fold(values, op):
    return op(values.reshape(values.shape[0] // 8, 8, values.shape[1]), axis=0)


def prefix_kernel(base, block, chunk, n_units, meta_ref, own_q_ref, other_q_ref, *refs):
    units = refs[:n_units]
    (own_out, own_lse, other_out), scratch = refs[n_units : n_units + 3], refs[n_units + 3 :]
    kv, q_buf, o_buf, l_buf, s_a, s_b, m_a, m_b, sems = scratch
    first_len = meta_ref[4] - base
    share = units[0].shape[2]

    def landing(job):
        return kv.at[job // 2, :, :, pl.ds((job % 2) * share, share)]

    for job in range(4):
        for unit in range(n_units):

            @pl.when(meta_ref[job] == unit)
            def _():
                pltpu.make_async_copy(units[unit], landing(job), sems.at[job]).start()

    columns, rows = own_out.shape
    q_buf[:columns] = own_q_ref[:, base : base + rows]
    q_buf[columns:] = other_q_ref[:, base : base + rows]
    for job in range(4):
        pltpu.make_async_copy(units[0], landing(job), sems.at[job]).wait()

    heads = columns // HEAD_SIZE
    per = 2 * heads
    keys = 2 * share
    parts = rows // block
    inside = jnp.clip(first_len, 0, rows)
    n_first = (inside + block - 1) // block
    skipped = inside // block
    pairs = n_first + parts - skipped

    def place(task):
        pair = task // per
        head = task % per
        second = (pair >= n_first).astype(jnp.int32)
        part = jnp.where(second == 1, pair - n_first + skipped, pair)
        cols = pl.ds(pl.multiple_of(part * block, block), block)
        q_band = pl.ds(pl.multiple_of(head * HEAD_SIZE, HEAD_SIZE), HEAD_SIZE)
        k_band = pl.ds(pl.multiple_of((head % heads) * HEAD_SIZE, HEAD_SIZE), HEAD_SIZE)
        return second, part, cols, q_band, k_band, head

    def step(now, later, s_now, m_now, s_later, m_later):
        if now is not None:
            second, part, cols, q_band, k_band, head = place(now)
            peak = m_now[...]
        later_second, _, later_cols, later_q, later_k, _ = place(later)
        query = q_buf[later_q, later_cols]
        top = total = blended = None
        for start in range(0, keys, chunk):
            span = pl.ds(start, chunk)
            scores = tn_dot(kv[later_second, 0, later_k, span], query)
            s_later[span, :] = scores
            folded = fold(scores, jnp.max)
            top = folded if top is None else jnp.maximum(top, folded)
            if now is not None:
                weights = jnp.exp(s_now[span, :] - peak)
                folded = fold(weights, jnp.sum)
                total = folded if total is None else total + folded
                out = nn_dot(kv[second, 1, k_band, span], weights.astype(jnp.bfloat16))
                blended = out if blended is None else blended + out
        m_later[...] = jnp.max(top, axis=0, keepdims=True)
        if now is not None:
            total = jnp.sum(total, axis=0, keepdims=True)
            lane = lax.broadcasted_iota(jnp.int32, (1, block), 1) + part * block
            mine = (lane >= first_len).astype(jnp.int32) == second
            o_buf[q_band, cols] = jnp.where(mine, blended * (1.0 / total), o_buf[q_band, cols])
            l_buf[head, :, cols] = jnp.where(mine, peak + jnp.log(total), l_buf[head, :, cols])

    step(None, 0, None, None, s_a, m_a)

    def two(index, carry):
        task = 2 * index
        step(task, task + 1, s_a, m_a, s_b, m_b)
        step(task + 1, jnp.minimum(task + 2, pairs * per - 1), s_b, m_b, s_a, m_a)
        return carry

    lax.fori_loop(0, pairs * heads, two, 0)
    own_out[...] = o_buf[:columns]
    other_out[:columns] = o_buf[columns:].astype(jnp.bfloat16)
    for head in range(heads):
        own_lse[head : head + 1] = l_buf[head]
    rest = jnp.concatenate([l_buf[heads + head] for head in range(heads)] + [jnp.zeros((8 - heads, rows), jnp.float32)])
    terms = []
    for _ in range(3):
        terms.append(rest.astype(jnp.bfloat16).astype(jnp.float32))
        rest = rest - terms[-1]
    terms.append(jnp.zeros_like(rest))
    other_out[columns:] = jnp.concatenate(terms).astype(jnp.bfloat16)


def prefix_attend(meta, own_q, other_q, units, base, rows):
    columns = own_q.shape[0]
    share = units[0].shape[2]
    block = 128
    vmem = pl.BlockSpec(memory_space=pltpu.VMEM)
    out = jax.ShapeDtypeStruct((columns, rows), jnp.float32)
    lse = jax.ShapeDtypeStruct((8, rows), jnp.float32)
    sent = jax.ShapeDtypeStruct((columns + 32, rows), jnp.bfloat16)
    return pl.pallas_call(
        functools.partial(prefix_kernel, base, block, 256, len(units)),
        out_shape=(out, lse, sent),
        in_specs=[pl.BlockSpec(memory_space=pltpu.SMEM), vmem, vmem]
        + [pl.BlockSpec(memory_space=pl.ANY)] * len(units),
        out_specs=[vmem] * 3,
        scratch_shapes=[
            pltpu.VMEM((2, 2, columns, 2 * share), jnp.bfloat16),
            pltpu.VMEM((2 * columns, rows), jnp.bfloat16),
            pltpu.VMEM((2 * columns, rows), jnp.float32),
            pltpu.VMEM((16, 1, rows), jnp.float32),
            pltpu.VMEM((2 * share, block), jnp.float32),
            pltpu.VMEM((2 * share, block), jnp.float32),
            pltpu.VMEM((1, block), jnp.float32),
            pltpu.VMEM((1, block), jnp.float32),
            pltpu.SemaphoreType.DMA((4,)),
        ],
        cost_estimate=pl.CostEstimate(
            flops=32 * columns * rows * share, bytes_accessed=6 << 20, transcendentals=20 * rows * share
        ),
        name="prefix_attend",
    )(meta, own_q, other_q, *units)


def merge_kernel(own_ref, own_lse_ref, got_ref, suffix_ref, suffix_lse_ref, out_ref):
    columns = own_ref.shape[0]
    packed = got_ref[columns:].astype(jnp.float32)
    got_lse = packed[:8] + packed[8:16] + packed[16:24]
    lses = [own_lse_ref[...], got_lse, suffix_lse_ref[...]]
    for head in range(columns // HEAD_SIZE):
        band = pl.ds(head * HEAD_SIZE, HEAD_SIZE)
        parts = [lse[head : head + 1] for lse in lses]
        top = jnp.maximum(jnp.maximum(parts[0], parts[1]), parts[2])
        factors = [jnp.exp(part - top) for part in parts]
        share = 1.0 / (factors[0] + factors[1] + factors[2])
        out_ref[band] = (
            own_ref[band] * (factors[0] * share)
            + got_ref[band].astype(jnp.float32) * (factors[1] * share)
            + suffix_ref[band] * (factors[2] * share)
        ).astype(jnp.bfloat16)


def merge(own, own_lse, got, suffix, suffix_lse, index):
    columns, rows = own.shape
    return pl.pallas_call(
        merge_kernel,
        out_shape=jax.ShapeDtypeStruct((columns, rows), jnp.bfloat16),
        grid=(1,),
        in_specs=[
            pl.BlockSpec((columns, rows), lambda i: (0, 0)),
            pl.BlockSpec((8, rows), lambda i: (0, 0)),
            pl.BlockSpec((columns + 32, rows), lambda i: (0, 0)),
            pl.BlockSpec((columns, rows), lambda i: (0, index)),
            pl.BlockSpec((8, rows), lambda i: (0, index)),
        ],
        out_specs=pl.BlockSpec((columns, rows), lambda i: (0, 0)),
        cost_estimate=pl.CostEstimate(flops=8 * columns * rows, bytes_accessed=1 << 20, transcendentals=15 * rows),
        name="merge",
    )(own, own_lse, got, suffix, suffix_lse)


def local(
    n_req,
    tokens,
    owners,
    request_groups,
    request_lengths,
    prefix_cache,
    attn_gain,
    query_weight,
    key_value_weight,
    query_gain,
    key_gain,
    w_out,
    ffn_gain,
    w_gate_up,
    w_down,
):
    row_count, width = tokens.shape
    columns = query_weight.shape[1]
    head_count = columns // HEAD_SIZE
    rank = lax.axis_index("tp")
    my_req = lax.axis_index("req")
    core = rank % 2

    def across_chip(value):
        return lax.ppermute(value, "tp", [(i, i ^ 2) for i in range(4)])

    def across_core(value):
        return lax.ppermute(value, "tp", [(i, i ^ 1) for i in range(4)])

    length = n_req // 2
    share = prefix_cache.shape[2] // 2
    mine = lax.dynamic_slice_in_dim(jnp.transpose(prefix_cache[0], (0, 2, 1)), core * share, share, 2)

    def ring(value):
        return lax.ppermute(value, "req", [(r, (r + 2) % n_req) for r in range(n_req)])

    def aside(value):
        return lax.ppermute(value, "req", [(r, r ^ 1) for r in range(n_req)])

    held = [mine, ring(mine)]
    units = [mine, aside(mine)]
    wanted = owners.reshape(-1, 2)[request_groups[0]].reshape(-1)
    distance = (my_req // 2 - wanted // 2) % length
    unit_index = 2 * distance + (wanted % 2 != my_req % 2).astype(jnp.int32)

    from_chip = across_chip(tokens)
    from_core = across_core(tokens)
    from_both = across_core(from_chip)
    w_gate, w_up = w_gate_up[:, 0], w_gate_up[:, 1]
    pieces, w_gate, w_up, _ = lax.optimization_barrier(
        ((tokens, from_core, from_chip, from_both), w_gate, w_up, held[1])
    )
    full_rows, normalized_input = gather_norm(rank, pieces, attn_gain)

    w_out_held, _ = lax.optimization_barrier((w_out, from_chip))
    w_out_chip = across_chip(w_out_held)
    w_out_core = across_core(w_out)
    w_out_both = across_core(w_out_chip)
    w_out_all = jnp.concatenate([w_out, w_out_core, w_out_chip, w_out_both], axis=0)

    row_index = jnp.arange(row_count, dtype=jnp.int32)
    first_len = request_lengths[0, 0]
    segment = (row_index >= first_len).astype(jnp.int32)
    position = row_index - segment * first_len + PREFIX
    query_rows = jnp.dot(
        normalized_input, query_weight, preferred_element_type=jnp.float32
    ).reshape(row_count, head_count, HEAD_SIZE)
    key_value_rows = jnp.dot(
        normalized_input, key_value_weight, preferred_element_type=jnp.float32
    ).reshape(row_count, 2, head_count, HEAD_SIZE)
    query_rows, key_value_rows, second = lax.optimization_barrier((query_rows, key_value_rows, ring(held[1])))
    units += [held[1], aside(held[1]), second, aside(second)]
    held.append(second)
    for _ in range(3, length):
        held.append(ring(held[-1]))
        units += [held[-1], aside(held[-1])]
    query_rows = rotate(rms_scale(query_rows, query_gain), position).astype(jnp.bfloat16)
    key_rows = rotate(rms_scale(key_value_rows[:, 0], key_gain), position).astype(jnp.bfloat16)
    value_rows = key_value_rows[:, 1].astype(jnp.bfloat16)
    cache_rows = jnp.stack(
        [key_rows.reshape(row_count, columns), value_rows.reshape(row_count, columns)],
        axis=1,
    )
    own_q = (query_rows * HEAD_SIZE**-0.5).reshape(row_count, columns).T
    other_q = across_core(own_q)
    suffix_out, suffix_lse = suffix_attend(
        first_len, own_q, key_rows.reshape(row_count, columns).T, value_rows.reshape(row_count, columns).T
    )

    own_q, suffix_out, suffix_lse = lax.optimization_barrier((own_q, suffix_out, suffix_lse))
    meta = jnp.concatenate([unit_index.astype(jnp.int32), first_len.reshape(1)])
    def block_of(value, flip):
        return lax.dynamic_slice_in_dim(value, (rank ^ flip) * width, width, 1)

    chunk = row_count // 2
    gathered = []
    for base in range(0, row_count, chunk):
        own_out, own_lse, sent = prefix_attend(meta, own_q, other_q, units, base, chunk)
        attention = merge(own_out, own_lse, across_core(sent), suffix_out, suffix_lse, base // chunk)
        att_chip = across_chip(attention)
        gathered.append([attention, across_core(attention), att_chip, across_core(att_chip)])

    hidden = []
    far_sum = None
    for index, parts in enumerate(gathered):
        if far_sum is not None:
            parts, far_sum = lax.optimization_barrier((parts, far_sum))
            got_chip = across_chip(far_sum)
        head_total = tn_dot(jnp.concatenate(parts, axis=0), w_out_all)
        mixed = full_rows[index * chunk : (index + 1) * chunk].astype(jnp.float32) + head_total
        normed_ffn = rms_scale(mixed, ffn_gain).astype(jnp.bfloat16)
        gate = jnp.dot(normed_ffn, w_gate, preferred_element_type=jnp.float32)
        up = jnp.dot(normed_ffn, w_up, preferred_element_type=jnp.float32)
        activated = (jax.nn.silu(gate) * up).astype(jnp.bfloat16)
        if far_sum is not None:
            activated, got_chip = lax.optimization_barrier((activated, got_chip))
            hidden.append((near_sum + got_chip.astype(jnp.float32)).astype(jnp.bfloat16))
        down_part = jnp.dot(activated, w_down, preferred_element_type=jnp.float32).astype(jnp.bfloat16)
        got_far = across_core(block_of(down_part, 3))
        got_near = across_core(block_of(down_part, 1))
        far_sum = (block_of(down_part, 2).astype(jnp.float32) + got_far.astype(jnp.float32)).astype(jnp.bfloat16)
        near_sum = block_of(mixed, 0) + block_of(down_part, 0).astype(jnp.float32) + got_near.astype(jnp.float32)
    hidden.append((near_sum + across_chip(far_sum).astype(jnp.float32)).astype(jnp.bfloat16))
    return (jnp.concatenate(hidden, axis=0), cache_rows)


def solution(mesh):
    placed = (
        P("req", "tp"),
        P(),
        P("req", None),
        P("req", None),
        P("req", None, None, None),
        P(),
        P(None, "tp"),
        P(),
        P(),
        P(),
        P("tp", None),
        P(),
        P(None, None, "tp"),
        P("tp", None),
    )
    return jax.shard_map(
        functools.partial(local, mesh.shape["req"]),
        mesh=mesh,
        in_specs=placed,
        out_specs=(P("req", "tp"), P("req", None, None)),
        check_vma=False,
    )
```

```python
import functools

import jax
import jax.numpy as jnp
from jax import lax
from jax.experimental import pallas as pl
from jax.experimental.pallas import tpu as pltpu
from jax.sharding import PartitionSpec as P

HEAD_SIZE = 64
PREFIX = 1536

eps_norm = 1e-06
rope_base = 10000.0
masked_score = -1e30
VMEM_LIMIT = 60 * 1024 * 1024


def rms_scale(values, gain_vec):
    mean_sq = jnp.mean(values * values, axis=-1, keepdims=True)
    return values * lax.rsqrt(mean_sq + eps_norm) * gain_vec


def rotate(values, positions):
    half_size = values.shape[-1] // 2
    frequency = rope_base ** (-jnp.arange(half_size, dtype=jnp.float32) * 2.0 / values.shape[-1])
    angles = positions.astype(jnp.float32)[:, None] * frequency[None, :]
    cos_part = jnp.cos(angles)[:, None, :]
    sin_part = jnp.sin(angles)[:, None, :]
    front_half = values[..., :half_size]
    back_half = values[..., half_size:]
    return jnp.concatenate(
        [
            front_half * cos_part - back_half * sin_part,
            back_half * cos_part + front_half * sin_part,
        ],
        axis=-1,
    )


def tn_dot(lhs, rhs):
    return lax.dot_general(lhs, rhs, (((0,), (0,)), ((), ())), preferred_element_type=jnp.float32)


def nn_dot(lhs, rhs):
    return lax.dot_general(lhs, rhs, (((1,), (0,)), ((), ())), preferred_element_type=jnp.float32)


def norm_kernel(rank_ref, own_ref, core_ref, chip_ref, both_ref, gain_ref, full_ref, normed_ref):
    rank = rank_ref[0]
    width = own_ref.shape[1]
    pieces = [own_ref, core_ref, chip_ref, both_ref]
    values = [piece[...].astype(jnp.float32) for piece in pieces]
    total = sum(jnp.sum(v * v, axis=-1, keepdims=True) for v in values)
    scale = lax.rsqrt(total / full_ref.shape[1] + eps_norm)
    for flip, (piece, value) in enumerate(zip(pieces, values)):
        place = pl.multiple_of((rank ^ flip) * width, width)
        columns = pl.ds(place, width)
        full_ref[:, columns] = piece[...]
        normed_ref[:, columns] = (value * scale * gain_ref[:, columns]).astype(jnp.bfloat16)


def gather_norm(rank, pieces, gain):
    rows, width = pieces[0].shape
    block = 128
    full = width * len(pieces)
    piece_spec = pl.BlockSpec((block, width), lambda i, s: (i, 0))
    full_spec = pl.BlockSpec((block, full), lambda i, s: (i, 0))
    return pl.pallas_call(
        norm_kernel,
        out_shape=(
            jax.ShapeDtypeStruct((rows, full), jnp.bfloat16),
            jax.ShapeDtypeStruct((rows, full), jnp.bfloat16),
        ),
        grid_spec=pltpu.PrefetchScalarGridSpec(
            num_scalar_prefetch=1,
            grid=(rows // block,),
            in_specs=[piece_spec] * 4 + [pl.BlockSpec((1, full), lambda i, s: (0, 0))],
            out_specs=[full_spec, full_spec],
        ),
        name="gather_norm",
    )(rank.reshape(1), *pieces, gain.reshape(1, full))


def suffix_kernel(len_ref, q_ref, k_ref, v_ref, out_ref, lse_ref):
    first_len = len_ref[0]
    rows = q_ref.shape[1]
    block = 256
    heads = q_ref.shape[0] // HEAD_SIZE
    for start in range(0, rows, block):
        keys = start + block
        key_index = lax.broadcasted_iota(jnp.int32, (keys, block), 0)
        row_index = lax.broadcasted_iota(jnp.int32, (keys, block), 1) + start
        begin = jnp.where(row_index >= first_len, first_len, 0)
        allowed = (key_index <= row_index) & (key_index >= begin)
        for head in range(heads):
            band = pl.ds(head * HEAD_SIZE, HEAD_SIZE)
            scores = tn_dot(k_ref[band, :keys], q_ref[band, start : start + block])
            scores = jnp.where(allowed, scores, masked_score)
            row_max = jnp.max(scores, axis=0, keepdims=True)
            weights = jnp.exp(scores - row_max)
            total = jnp.sum(weights, axis=0, keepdims=True)
            blended = nn_dot(v_ref[band, :keys], weights.astype(jnp.bfloat16))
            out_ref[band, start : start + block] = blended / total
            lse_ref[head : head + 1, start : start + block] = row_max + jnp.log(total)


def suffix_attend(first_len, q_t, k_t, v_t):
    columns, rows = q_t.shape
    vmem = pl.BlockSpec(memory_space=pltpu.VMEM)
    return pl.pallas_call(
        suffix_kernel,
        out_shape=(
            jax.ShapeDtypeStruct((columns, rows), jnp.float32),
            jax.ShapeDtypeStruct((8, rows), jnp.float32),
        ),
        in_specs=[pl.BlockSpec(memory_space=pltpu.SMEM), vmem, vmem, vmem],
        out_specs=[vmem, vmem],
        cost_estimate=pl.CostEstimate(flops=4 * columns * rows * rows, bytes_accessed=3 << 20, transcendentals=5 * rows * rows),
        name="suffix_attend",
    )(first_len.reshape(1), q_t, k_t, v_t)


def fold(values, op):
    return op(values.reshape(values.shape[0] // 8, 8, values.shape[1]), axis=0)


def prefix_kernel(block, chunk, n_units, meta_ref, own_q_ref, other_q_ref, *refs):
    units, last_keys, last_values = refs[: n_units - 1], refs[n_units - 1], refs[n_units]
    (own_out, own_lse, other_out), scratch = refs[n_units + 1 : n_units + 4], refs[n_units + 4 :]
    kv, q_buf, o_buf, l_buf, s_a, s_b, m_a, m_b, sems = scratch
    first_len = meta_ref[4]
    share = units[0].shape[2]

    def landing(job, kind=slice(None)):
        return kv.at[job // 2, kind, :, pl.ds((job % 2) * share, share)]

    for job in range(4):
        for unit in range(n_units - 1):

            @pl.when(meta_ref[job] == unit)
            def _():
                pltpu.make_async_copy(units[unit], landing(job), sems.at[job]).start()

        @pl.when(meta_ref[job] == n_units - 1)
        def _():
            pltpu.make_async_copy(last_keys, landing(job, pl.ds(0, 1)), sems.at[job]).start()
            pltpu.make_async_copy(last_values, landing(job, pl.ds(1, 1)), sems.at[job]).start()

    columns, rows = own_out.shape
    q_buf[:columns] = own_q_ref[...]
    q_buf[columns:] = other_q_ref[...]
    for job in range(4):
        pltpu.make_async_copy(units[0], landing(job), sems.at[job]).wait()

    heads = columns // HEAD_SIZE
    per = 2 * heads
    keys = 2 * share
    parts = rows // block
    inside = jnp.clip(first_len, 0, rows)
    n_first = (inside + block - 1) // block
    skipped = inside // block
    pairs = n_first + parts - skipped

    def place(task):
        pair = task // per
        head = task % per
        second = (pair >= n_first).astype(jnp.int32)
        part = jnp.where(second == 1, pair - n_first + skipped, pair)
        cols = pl.ds(pl.multiple_of(part * block, block), block)
        q_band = pl.ds(pl.multiple_of(head * HEAD_SIZE, HEAD_SIZE), HEAD_SIZE)
        k_band = pl.ds(pl.multiple_of((head % heads) * HEAD_SIZE, HEAD_SIZE), HEAD_SIZE)
        return second, part, cols, q_band, k_band, head

    def step(now, later, s_now, m_now, s_later, m_later):
        if now is not None:
            second, part, cols, q_band, k_band, head = place(now)
            peak = m_now[...]
        later_second, _, later_cols, later_q, later_k, _ = place(later)
        query = q_buf[later_q, later_cols]
        top = total = blended = None
        for start in range(0, keys, chunk):
            span = pl.ds(start, chunk)
            scores = tn_dot(kv[later_second, 0, later_k, span], query)
            s_later[span, :] = scores
            folded = fold(scores, jnp.max)
            top = folded if top is None else jnp.maximum(top, folded)
            if now is not None:
                weights = jnp.exp(s_now[span, :] - peak)
                folded = fold(weights, jnp.sum)
                total = folded if total is None else total + folded
                out = nn_dot(kv[second, 1, k_band, span], weights.astype(jnp.bfloat16))
                blended = out if blended is None else blended + out
        m_later[...] = jnp.max(top, axis=0, keepdims=True)
        if now is not None:
            total = jnp.sum(total, axis=0, keepdims=True)
            lane = lax.broadcasted_iota(jnp.int32, (1, block), 1) + part * block
            mine = (lane >= first_len).astype(jnp.int32) == second
            o_buf[q_band, cols] = jnp.where(mine, blended * (1.0 / total), o_buf[q_band, cols])
            l_buf[head, :, cols] = jnp.where(mine, peak + jnp.log(total), l_buf[head, :, cols])

    step(None, 0, None, None, s_a, m_a)

    def two(index, carry):
        task = 2 * index
        step(task, task + 1, s_a, m_a, s_b, m_b)
        step(task + 1, jnp.minimum(task + 2, pairs * per - 1), s_b, m_b, s_a, m_a)
        return carry

    lax.fori_loop(0, pairs * heads, two, 0)
    own_out[...] = o_buf[:columns]
    other_out[:columns] = o_buf[columns:].astype(jnp.bfloat16)
    for head in range(heads):
        own_lse[head : head + 1] = l_buf[head]
    rest = jnp.concatenate([l_buf[heads + head] for head in range(heads)] + [jnp.zeros((8 - heads, rows), jnp.float32)])
    terms = []
    for _ in range(3):
        terms.append(rest.astype(jnp.bfloat16).astype(jnp.float32))
        rest = rest - terms[-1]
    terms.append(jnp.zeros_like(rest))
    other_out[columns:] = jnp.concatenate(terms).astype(jnp.bfloat16)


def prefix_attend(meta, own_q, other_q, units):
    columns, rows = own_q.shape
    share = units[0].shape[2]
    block = 256
    vmem = pl.BlockSpec(memory_space=pltpu.VMEM)
    out = jax.ShapeDtypeStruct((columns, rows), jnp.float32)
    lse = jax.ShapeDtypeStruct((8, rows), jnp.float32)
    sent = jax.ShapeDtypeStruct((columns + 32, rows), jnp.bfloat16)
    return pl.pallas_call(
        functools.partial(prefix_kernel, block, 256, len(units) - 1),
        out_shape=(out, lse, sent),
        in_specs=[pl.BlockSpec(memory_space=pltpu.SMEM), vmem, vmem]
        + [pl.BlockSpec(memory_space=pl.ANY)] * len(units),
        out_specs=[vmem] * 3,
        scratch_shapes=[
            pltpu.VMEM((2, 2, columns, 2 * share), jnp.bfloat16),
            pltpu.VMEM((2 * columns, rows), jnp.bfloat16),
            pltpu.VMEM((2 * columns, rows), jnp.float32),
            pltpu.VMEM((16, 1, rows), jnp.float32),
            pltpu.VMEM((2 * share, block), jnp.float32),
            pltpu.VMEM((2 * share, block), jnp.float32),
            pltpu.VMEM((1, block), jnp.float32),
            pltpu.VMEM((1, block), jnp.float32),
            pltpu.SemaphoreType.DMA((4,)),
        ],
        cost_estimate=pl.CostEstimate(
            flops=32 * columns * rows * share, bytes_accessed=6 << 20, transcendentals=20 * rows * share
        ),
        name="prefix_attend",
    )(meta, own_q, other_q, *units)


def merge_kernel(own_ref, own_lse_ref, got_ref, suffix_ref, suffix_lse_ref, out_ref):
    columns = own_ref.shape[0]
    packed = got_ref[columns:].astype(jnp.float32)
    got_lse = packed[:8] + packed[8:16] + packed[16:24]
    lses = [own_lse_ref[...], got_lse, suffix_lse_ref[...]]
    for head in range(columns // HEAD_SIZE):
        band = pl.ds(head * HEAD_SIZE, HEAD_SIZE)
        parts = [lse[head : head + 1] for lse in lses]
        top = jnp.maximum(jnp.maximum(parts[0], parts[1]), parts[2])
        factors = [jnp.exp(part - top) for part in parts]
        share = 1.0 / (factors[0] + factors[1] + factors[2])
        out_ref[band] = (
            own_ref[band] * (factors[0] * share)
            + got_ref[band].astype(jnp.float32) * (factors[1] * share)
            + suffix_ref[band] * (factors[2] * share)
        ).astype(jnp.bfloat16)


def merge(own, own_lse, got, suffix, suffix_lse):
    columns, rows = own.shape
    return pl.pallas_call(
        merge_kernel,
        out_shape=jax.ShapeDtypeStruct((columns, rows), jnp.bfloat16),
        grid=(rows // 256,),
        in_specs=[
            pl.BlockSpec((columns, 256), lambda i: (0, i)),
            pl.BlockSpec((8, 256), lambda i: (0, i)),
            pl.BlockSpec((columns + 32, 256), lambda i: (0, i)),
            pl.BlockSpec((columns, 256), lambda i: (0, i)),
            pl.BlockSpec((8, 256), lambda i: (0, i)),
        ],
        out_specs=pl.BlockSpec((columns, 256), lambda i: (0, i)),
        cost_estimate=pl.CostEstimate(flops=8 * columns * rows, bytes_accessed=1 << 20, transcendentals=15 * rows),
        name="merge",
    )(own, own_lse, got, suffix, suffix_lse)


def local(
    n_req,
    tokens,
    owners,
    request_groups,
    request_lengths,
    prefix_cache,
    attn_gain,
    query_weight,
    key_value_weight,
    query_gain,
    key_gain,
    w_out,
    ffn_gain,
    w_gate_up,
    w_down,
):
    row_count, width = tokens.shape
    columns = query_weight.shape[1]
    head_count = columns // HEAD_SIZE
    rank = lax.axis_index("tp")
    my_req = lax.axis_index("req")
    core = rank % 2

    def across_chip(value):
        return lax.ppermute(value, "tp", [(i, i ^ 2) for i in range(4)])

    def across_core(value):
        return lax.ppermute(value, "tp", [(i, i ^ 1) for i in range(4)])

    length = n_req // 2
    share = prefix_cache.shape[2] // 2
    mine = lax.dynamic_slice_in_dim(jnp.transpose(prefix_cache[0], (0, 2, 1)), core * share, share, 2)

    def ring(value):
        return lax.ppermute(value, "req", [(r, (r + 2) % n_req) for r in range(n_req)])

    def aside(value):
        return lax.ppermute(value, "req", [(r, r ^ 1) for r in range(n_req)])

    held = [mine, ring(mine)]
    units = [mine, aside(mine)]
    wanted = owners.reshape(-1, 2)[request_groups[0]].reshape(-1)
    distance = (my_req // 2 - wanted // 2) % length
    unit_index = 2 * distance + (wanted % 2 != my_req % 2).astype(jnp.int32)

    from_chip = across_chip(tokens)
    from_core = across_core(tokens)
    from_both = across_core(from_chip)
    down_blocks = [
        lax.dynamic_slice_in_dim(w_down, (rank ^ flip) * width, width, 1) for flip in range(4)
    ]
    pieces, down_blocks, _ = lax.optimization_barrier(
        ((tokens, from_core, from_chip, from_both), down_blocks, held[1])
    )
    full_rows, normalized_input = gather_norm(rank, pieces, attn_gain)

    w_out_held, _ = lax.optimization_barrier((w_out, from_chip))
    w_out_chip = across_chip(w_out_held)
    w_out_core = across_core(w_out)
    w_out_both = across_core(w_out_chip)

    row_index = jnp.arange(row_count, dtype=jnp.int32)
    first_len = request_lengths[0, 0]
    segment = (row_index >= first_len).astype(jnp.int32)
    position = row_index - segment * first_len + PREFIX
    query_rows = jnp.dot(
        normalized_input, query_weight, preferred_element_type=jnp.float32
    ).reshape(row_count, head_count, HEAD_SIZE)
    key_value_rows = jnp.dot(
        normalized_input, key_value_weight, preferred_element_type=jnp.float32
    ).reshape(row_count, 2, head_count, HEAD_SIZE)
    query_rows, key_value_rows, second = lax.optimization_barrier((query_rows, key_value_rows, ring(held[1])))
    units += [held[1], aside(held[1])]
    held.append(second)
    for _ in range(3, length):
        units += [held[-1], aside(held[-1])]
        held.append(ring(held[-1]))
    units += [held[-1], aside(held[-1][:1]), ring(units[-1][1:])]
    query_rows = rotate(rms_scale(query_rows, query_gain), position).astype(jnp.bfloat16)
    key_rows = rotate(rms_scale(key_value_rows[:, 0], key_gain), position).astype(jnp.bfloat16)
    value_rows = key_value_rows[:, 1].astype(jnp.bfloat16)
    cache_rows = jnp.stack(
        [key_rows.reshape(row_count, columns), value_rows.reshape(row_count, columns)],
        axis=1,
    )
    own_q = (query_rows * HEAD_SIZE**-0.5).reshape(row_count, columns).T
    other_q = across_core(own_q)
    suffix_out, suffix_lse = suffix_attend(
        first_len, own_q, key_rows.reshape(row_count, columns).T, value_rows.reshape(row_count, columns).T
    )

    own_q, suffix_out, suffix_lse = lax.optimization_barrier((own_q, suffix_out, suffix_lse))
    meta = jnp.concatenate([unit_index.astype(jnp.int32), first_len.reshape(1)])
    own_out, own_lse, sent = prefix_attend(meta, own_q, other_q, units)
    attention = merge(own_out, own_lse, across_core(sent), suffix_out, suffix_lse)
    att_chip = across_chip(attention)
    att_core = across_core(attention)
    near_total = full_rows.astype(jnp.float32) + tn_dot(attention, w_out) + tn_dot(att_core, w_out_core)
    near_total, att_chip = lax.optimization_barrier((near_total, att_chip))
    att_both = across_core(att_chip)
    mixed = near_total + tn_dot(att_chip, w_out_chip) + tn_dot(att_both, w_out_both)
    normed_ffn = rms_scale(mixed, ffn_gain).astype(jnp.bfloat16)
    gate_up = jnp.einsum("rd,dgf->rgf", normed_ffn, w_gate_up, preferred_element_type=jnp.float32)
    activated = (jax.nn.silu(gate_up[:, 0]) * gate_up[:, 1]).astype(jnp.bfloat16)

    def down(flip):
        return jnp.dot(activated, down_blocks[flip], preferred_element_type=jnp.float32).astype(jnp.bfloat16)

    far = down(3)
    far_sum = (down(2).astype(jnp.float32) + across_core(far).astype(jnp.float32)).astype(jnp.bfloat16)
    from_far = across_chip(far_sum)
    activated, far_sum = lax.optimization_barrier((activated, far_sum))
    near = down(1)
    own_mixed = lax.dynamic_slice_in_dim(mixed, rank * width, width, 1)
    near_sum = own_mixed + down(0).astype(jnp.float32) + across_core(near).astype(jnp.float32)
    return ((near_sum + from_far.astype(jnp.float32)).astype(jnp.bfloat16), cache_rows)


def solution(mesh):
    placed = (
        P("req", "tp"),
        P(),
        P("req", None),
        P("req", None),
        P("req", None, None, None),
        P(),
        P(None, "tp"),
        P(),
        P(),
        P(),
        P("tp", None),
        P(),
        P(None, None, "tp"),
        P("tp", None),
    )
    return jax.shard_map(
        functools.partial(local, mesh.shape["req"]),
        mesh=mesh,
        in_specs=placed,
        out_specs=(P("req", "tp"), P("req", None, None)),
        check_vma=False,
    )
```

```python
import functools

import jax
import jax.numpy as jnp
from jax import lax
from jax.experimental import pallas as pl
from jax.experimental.pallas import tpu as pltpu
from jax.sharding import PartitionSpec as P

HEAD_SIZE = 64
PREFIX = 1536

eps_norm = 1e-06
rope_base = 10000.0
masked_score = -1e30
VMEM_LIMIT = 60 * 1024 * 1024


def rms_scale(values, gain_vec):
    mean_sq = jnp.mean(values * values, axis=-1, keepdims=True)
    return values * lax.rsqrt(mean_sq + eps_norm) * gain_vec


def turns(positions, half_size):
    frequency = rope_base ** (-jnp.arange(half_size, dtype=jnp.float32) * 2.0 / (2 * half_size))
    angles = positions.astype(jnp.float32)[:, None] * frequency[None, :]
    return jnp.cos(angles), jnp.sin(angles)


def rotate(values, cos_part, sin_part):
    half_size = values.shape[-1] // 2
    cos_part = cos_part[:, None, :]
    sin_part = sin_part[:, None, :]
    front_half = values[..., :half_size]
    back_half = values[..., half_size:]
    return jnp.concatenate(
        [
            front_half * cos_part - back_half * sin_part,
            back_half * cos_part + front_half * sin_part,
        ],
        axis=-1,
    )


def tn_dot(lhs, rhs):
    return lax.dot_general(lhs, rhs, (((0,), (0,)), ((), ())), preferred_element_type=jnp.float32)


def nn_dot(lhs, rhs):
    return lax.dot_general(lhs, rhs, (((1,), (0,)), ((), ())), preferred_element_type=jnp.float32)


def norm_kernel(rank_ref, own_ref, core_ref, chip_ref, both_ref, gain_ref, full_ref, normed_ref):
    rank = rank_ref[0]
    width = own_ref.shape[1]
    pieces = [own_ref, core_ref, chip_ref, both_ref]
    values = [piece[...].astype(jnp.float32) for piece in pieces]
    total = sum(jnp.sum(v * v, axis=-1, keepdims=True) for v in values)
    scale = lax.rsqrt(total / full_ref.shape[1] + eps_norm)
    for flip, (piece, value) in enumerate(zip(pieces, values)):
        place = pl.multiple_of((rank ^ flip) * width, width)
        columns = pl.ds(place, width)
        full_ref[:, columns] = piece[...]
        normed_ref[:, columns] = (value * scale * gain_ref[:, columns]).astype(jnp.bfloat16)


def gather_norm(rank, pieces, gain):
    rows, width = pieces[0].shape
    block = 128
    full = width * len(pieces)
    piece_spec = pl.BlockSpec((block, width), lambda i, s: (i, 0))
    full_spec = pl.BlockSpec((block, full), lambda i, s: (i, 0))
    return pl.pallas_call(
        norm_kernel,
        out_shape=(
            jax.ShapeDtypeStruct((rows, full), jnp.bfloat16),
            jax.ShapeDtypeStruct((rows, full), jnp.bfloat16),
        ),
        grid_spec=pltpu.PrefetchScalarGridSpec(
            num_scalar_prefetch=1,
            grid=(rows // block,),
            in_specs=[piece_spec] * 4 + [pl.BlockSpec((1, full), lambda i, s: (0, 0))],
            out_specs=[full_spec, full_spec],
        ),
        name="gather_norm",
    )(rank.reshape(1), *pieces, gain.reshape(1, full))


def suffix_kernel(len_ref, q_ref, k_ref, v_ref, out_ref, lse_ref):
    first_len = len_ref[0, 0]
    rows = q_ref.shape[1]
    block = 256
    heads = q_ref.shape[0] // HEAD_SIZE
    for start in range(0, rows, block):
        keys = start + block
        key_index = lax.broadcasted_iota(jnp.int32, (keys, block), 0)
        row_index = lax.broadcasted_iota(jnp.int32, (keys, block), 1) + start
        begin = jnp.where(row_index >= first_len, first_len, 0)
        allowed = (key_index <= row_index) & (key_index >= begin)
        for head in range(heads):
            band = pl.ds(head * HEAD_SIZE, HEAD_SIZE)
            scores = tn_dot(k_ref[band, :keys], q_ref[band, start : start + block])
            scores = jnp.where(allowed, scores, masked_score)
            row_max = jnp.max(scores, axis=0, keepdims=True)
            weights = jnp.exp(scores - row_max)
            total = jnp.sum(weights, axis=0, keepdims=True)
            blended = nn_dot(v_ref[band, :keys], weights.astype(jnp.bfloat16))
            out_ref[band, start : start + block] = blended / total
            lse_ref[head : head + 1, start : start + block] = row_max + jnp.log(total)


def suffix_attend(lengths, q_t, k_t, v_t):
    columns, rows = q_t.shape
    vmem = pl.BlockSpec(memory_space=pltpu.VMEM)
    return pl.pallas_call(
        suffix_kernel,
        out_shape=(
            jax.ShapeDtypeStruct((columns, rows), jnp.float32),
            jax.ShapeDtypeStruct((8, rows), jnp.float32),
        ),
        in_specs=[pl.BlockSpec(memory_space=pltpu.SMEM), vmem, vmem, vmem],
        out_specs=[vmem, vmem],
        cost_estimate=pl.CostEstimate(flops=4 * columns * rows * rows, bytes_accessed=3 << 20, transcendentals=5 * rows * rows),
        name="suffix_attend",
    )(lengths, q_t, k_t, v_t)


def fold(values, op):
    return op(values.reshape(values.shape[0] // 8, 8, values.shape[1]), axis=0)


def turn(place, length):
    return jnp.where(place % 2 == 0, place // 2, length - (place + 1) // 2)


def prefix_kernel(block, chunk, n_units, owners_ref, groups_ref, lengths_ref, me_ref, own_q_ref, other_q_ref, *refs):
    units, last_keys, last_values = refs[: n_units - 1], refs[n_units - 1], refs[n_units]
    (own_out, own_lse, other_out), scratch = refs[n_units + 1 : n_units + 4], refs[n_units + 4 :]
    kv, q_buf, o_buf, l_buf, s_a, s_b, m_a, m_b, sems = scratch
    first_len = lengths_ref[0, 0]
    me = me_ref[0]
    length = n_units // 2
    share = units[0].shape[2]

    def landing(job, kind=slice(None)):
        return kv.at[job // 2, kind, :, pl.ds((job % 2) * share, share)]

    for job in range(4):
        holder = owners_ref[2 * groups_ref[0, job // 2] + job % 2]
        away = turn(me // 2, length) - turn(holder // 2, length)
        away = jnp.where(away < 0, away + length, away)
        wanted = 2 * away + jnp.where(holder % 2 == me % 2, 0, 1)
        for unit in range(n_units - 1):

            @pl.when(wanted == unit)
            def _():
                pltpu.make_async_copy(units[unit], landing(job), sems.at[job]).start()

        @pl.when(wanted == n_units - 1)
        def _():
            pltpu.make_async_copy(last_keys, landing(job, pl.ds(0, 1)), sems.at[job]).start()
            pltpu.make_async_copy(last_values, landing(job, pl.ds(1, 1)), sems.at[job]).start()

    columns, rows = own_out.shape
    q_buf[:columns] = own_q_ref[...]
    q_buf[columns:] = other_q_ref[...]
    for job in range(4):
        pltpu.make_async_copy(units[0], landing(job), sems.at[job]).wait()

    heads = columns // HEAD_SIZE
    per = 2 * heads
    keys = 2 * share
    parts = rows // block
    inside = jnp.clip(first_len, 0, rows)
    n_first = (inside + block - 1) // block
    skipped = inside // block
    pairs = n_first + parts - skipped

    def place(task):
        pair = task // per
        head = task % per
        second = (pair >= n_first).astype(jnp.int32)
        part = jnp.where(second == 1, pair - n_first + skipped, pair)
        cols = pl.ds(pl.multiple_of(part * block, block), block)
        q_band = pl.ds(pl.multiple_of(head * HEAD_SIZE, HEAD_SIZE), HEAD_SIZE)
        k_band = pl.ds(pl.multiple_of((head % heads) * HEAD_SIZE, HEAD_SIZE), HEAD_SIZE)
        return second, part, cols, q_band, k_band, head

    def step(now, later, s_now, m_now, s_later, m_later):
        if now is not None:
            second, part, cols, q_band, k_band, head = place(now)
            peak = m_now[...]
        later_second, _, later_cols, later_q, later_k, _ = place(later)
        query = q_buf[later_q, later_cols]
        top = total = blended = None
        for start in range(0, keys, chunk):
            span = pl.ds(start, chunk)
            scores = tn_dot(kv[later_second, 0, later_k, span], query)
            s_later[span, :] = scores
            folded = fold(scores, jnp.max)
            top = folded if top is None else jnp.maximum(top, folded)
            if now is not None:
                weights = jnp.exp(s_now[span, :] - peak)
                folded = fold(weights, jnp.sum)
                total = folded if total is None else total + folded
                out = nn_dot(kv[second, 1, k_band, span], weights.astype(jnp.bfloat16))
                blended = out if blended is None else blended + out
        m_later[...] = jnp.max(top, axis=0, keepdims=True)
        if now is not None:
            total = jnp.sum(total, axis=0, keepdims=True)
            lane = lax.broadcasted_iota(jnp.int32, (1, block), 1) + part * block
            mine = (lane >= first_len).astype(jnp.int32) == second
            o_buf[q_band, cols] = jnp.where(mine, blended * (1.0 / total), o_buf[q_band, cols])
            l_buf[head, :, cols] = jnp.where(mine, peak + jnp.log(total), l_buf[head, :, cols])

    step(None, 0, None, None, s_a, m_a)

    def two(index, carry):
        task = 2 * index
        step(task, task + 1, s_a, m_a, s_b, m_b)
        step(task + 1, jnp.minimum(task + 2, pairs * per - 1), s_b, m_b, s_a, m_a)
        return carry

    lax.fori_loop(0, pairs * heads, two, 0)
    own_out[...] = o_buf[:columns]
    other_out[:columns] = o_buf[columns:].astype(jnp.bfloat16)
    for head in range(heads):
        own_lse[head : head + 1] = l_buf[head]
    rest = jnp.concatenate([l_buf[heads + head] for head in range(heads)] + [jnp.zeros((8 - heads, rows), jnp.float32)])
    terms = []
    for _ in range(3):
        terms.append(rest.astype(jnp.bfloat16).astype(jnp.float32))
        rest = rest - terms[-1]
    terms.append(jnp.zeros_like(rest))
    other_out[columns:] = jnp.concatenate(terms).astype(jnp.bfloat16)


def prefix_attend(owners, groups, lengths, me, own_q, other_q, units):
    columns, rows = own_q.shape
    share = units[0].shape[2]
    block = 256
    vmem = pl.BlockSpec(memory_space=pltpu.VMEM)
    out = jax.ShapeDtypeStruct((columns, rows), jnp.float32)
    lse = jax.ShapeDtypeStruct((8, rows), jnp.float32)
    sent = jax.ShapeDtypeStruct((columns + 32, rows), jnp.bfloat16)
    return pl.pallas_call(
        functools.partial(prefix_kernel, block, 256, len(units) - 1),
        out_shape=(out, lse, sent),
        in_specs=[pl.BlockSpec(memory_space=pltpu.SMEM)] * 4
        + [vmem] * 2
        + [pl.BlockSpec(memory_space=pl.ANY)] * len(units),
        out_specs=[vmem] * 3,
        scratch_shapes=[
            pltpu.VMEM((2, 2, columns, 2 * share), jnp.bfloat16),
            pltpu.VMEM((2 * columns, rows), jnp.bfloat16),
            pltpu.VMEM((2 * columns, rows), jnp.float32),
            pltpu.VMEM((16, 1, rows), jnp.float32),
            pltpu.VMEM((2 * share, block), jnp.float32),
            pltpu.VMEM((2 * share, block), jnp.float32),
            pltpu.VMEM((1, block), jnp.float32),
            pltpu.VMEM((1, block), jnp.float32),
            pltpu.SemaphoreType.DMA((4,)),
        ],
        cost_estimate=pl.CostEstimate(
            flops=32 * columns * rows * share, bytes_accessed=6 << 20, transcendentals=20 * rows * share
        ),
        name="prefix_attend",
    )(owners, groups, lengths, me, own_q, other_q, *units)


def merge_kernel(own_ref, own_lse_ref, got_ref, suffix_ref, suffix_lse_ref, out_ref):
    columns = own_ref.shape[0]
    packed = got_ref[columns:].astype(jnp.float32)
    got_lse = packed[:8] + packed[8:16] + packed[16:24]
    lses = [own_lse_ref[...], got_lse, suffix_lse_ref[...]]
    for head in range(columns // HEAD_SIZE):
        band = pl.ds(head * HEAD_SIZE, HEAD_SIZE)
        parts = [lse[head : head + 1] for lse in lses]
        top = jnp.maximum(jnp.maximum(parts[0], parts[1]), parts[2])
        factors = [jnp.exp(part - top) for part in parts]
        share = 1.0 / (factors[0] + factors[1] + factors[2])
        out_ref[band] = (
            own_ref[band] * (factors[0] * share)
            + got_ref[band].astype(jnp.float32) * (factors[1] * share)
            + suffix_ref[band] * (factors[2] * share)
        ).astype(jnp.bfloat16)


def merge(own, own_lse, got, suffix, suffix_lse):
    columns, rows = own.shape
    return pl.pallas_call(
        merge_kernel,
        out_shape=jax.ShapeDtypeStruct((columns, rows), jnp.bfloat16),
        grid=(rows // 256,),
        in_specs=[
            pl.BlockSpec((columns, 256), lambda i: (0, i)),
            pl.BlockSpec((8, 256), lambda i: (0, i)),
            pl.BlockSpec((columns + 32, 256), lambda i: (0, i)),
            pl.BlockSpec((columns, 256), lambda i: (0, i)),
            pl.BlockSpec((8, 256), lambda i: (0, i)),
        ],
        out_specs=pl.BlockSpec((columns, 256), lambda i: (0, i)),
        cost_estimate=pl.CostEstimate(flops=8 * columns * rows, bytes_accessed=1 << 20, transcendentals=15 * rows),
        name="merge",
    )(own, own_lse, got, suffix, suffix_lse)


def local(
    n_req,
    tokens,
    owners,
    request_groups,
    request_lengths,
    prefix_cache,
    attn_gain,
    query_weight,
    key_value_weight,
    query_gain,
    key_gain,
    w_out,
    ffn_gain,
    w_gate_up,
    w_down,
):
    row_count, width = tokens.shape
    columns = query_weight.shape[1]
    head_count = columns // HEAD_SIZE
    rank = lax.axis_index("tp")
    my_req = lax.axis_index("req")
    core = rank % 2

    def across_chip(value):
        return lax.ppermute(value, "tp", [(i, i ^ 2) for i in range(4)])

    def across_core(value):
        return lax.ppermute(value, "tp", [(i, i ^ 1) for i in range(4)])

    row_index = jnp.arange(row_count, dtype=jnp.int32)
    first_len = request_lengths[0, 0]
    segment = (row_index >= first_len).astype(jnp.int32)
    position = row_index - segment * first_len + PREFIX
    cos_part, sin_part = turns(position, HEAD_SIZE // 2)

    length = n_req // 2
    share = prefix_cache.shape[2] // 2
    mine = lax.dynamic_slice(jnp.transpose(prefix_cache[0], (0, 2, 1)), (0, 0, core * share), (2, columns, share))

    def ring(value):
        order = [*range(0, length, 2), *range(length - 1 - length % 2, 0, -2)]
        steps = zip(order, order[1:] + order[:1])
        return lax.ppermute(value, "req", [(2 * a + b, 2 * c + b) for a, c in steps for b in range(2)])

    def aside(value):
        return lax.ppermute(value, "req", [(r, r ^ 1) for r in range(n_req)])

    held = [mine, ring(mine)]
    units = [mine, aside(mine)]
    from_chip = across_chip(tokens)
    from_core = across_core(tokens)
    down_blocks = [
        lax.dynamic_slice_in_dim(w_down, (rank ^ flip) * width, width, 1) for flip in range(4)
    ]
    held[1], units[1], down_blocks, cos_part, sin_part = lax.optimization_barrier(
        (held[1], units[1], down_blocks, cos_part, sin_part)
    )
    from_chip, _ = lax.optimization_barrier((from_chip, held[1]))
    from_both = across_core(from_chip)
    full_rows, normalized_input = gather_norm(rank, (tokens, from_core, from_chip, from_both), attn_gain)

    w_out_held, _ = lax.optimization_barrier((w_out, from_chip))
    w_out_chip = across_chip(w_out_held)
    w_out_core = across_core(w_out)
    w_out_both = across_core(w_out_chip)

    query_rows = jnp.dot(
        normalized_input, query_weight, preferred_element_type=jnp.float32
    ).reshape(row_count, head_count, HEAD_SIZE)
    key_value_rows = jnp.dot(
        normalized_input, key_value_weight, preferred_element_type=jnp.float32
    ).reshape(row_count, 2, head_count, HEAD_SIZE)
    query_rows, key_value_rows, second = lax.optimization_barrier((query_rows, key_value_rows, ring(held[1])))
    units += [held[1], aside(held[1])]
    held.append(second)
    for _ in range(3, length):
        units += [held[-1], aside(held[-1])]
        held.append(ring(held[-1]))
    units += [held[-1], aside(held[-1][:1]), ring(units[-1][1:])]
    query_rows = rotate(rms_scale(query_rows, query_gain), cos_part, sin_part).astype(jnp.bfloat16)
    key_rows = rotate(rms_scale(key_value_rows[:, 0], key_gain), cos_part, sin_part).astype(jnp.bfloat16)
    value_rows = key_value_rows[:, 1].astype(jnp.bfloat16)
    cache_rows = jnp.stack(
        [key_rows.reshape(row_count, columns), value_rows.reshape(row_count, columns)],
        axis=1,
    )
    own_q = (query_rows * HEAD_SIZE**-0.5).reshape(row_count, columns).T
    other_q = across_core(own_q)
    suffix_out, suffix_lse = suffix_attend(
        request_lengths, own_q, key_rows.reshape(row_count, columns).T, value_rows.reshape(row_count, columns).T
    )

    own_q, suffix_out, suffix_lse = lax.optimization_barrier((own_q, suffix_out, suffix_lse))
    own_out, own_lse, sent = prefix_attend(
        owners, request_groups, request_lengths, my_req.reshape(1), own_q, other_q, units
    )
    attention = merge(own_out, own_lse, across_core(sent), suffix_out, suffix_lse)
    att_chip = across_chip(attention)
    att_core = across_core(attention)
    near_total = full_rows.astype(jnp.float32) + tn_dot(attention, w_out) + tn_dot(att_core, w_out_core)
    near_total, att_chip = lax.optimization_barrier((near_total, att_chip))
    att_both = across_core(att_chip)
    mixed = near_total + tn_dot(att_chip, w_out_chip) + tn_dot(att_both, w_out_both)
    normed_ffn = rms_scale(mixed, ffn_gain).astype(jnp.bfloat16)
    gate_up = jnp.einsum("rd,dgf->rgf", normed_ffn, w_gate_up, preferred_element_type=jnp.float32)
    activated = (jax.nn.silu(gate_up[:, 0]) * gate_up[:, 1]).astype(jnp.bfloat16)

    def down(flip):
        return jnp.dot(activated, down_blocks[flip], preferred_element_type=jnp.float32).astype(jnp.bfloat16)

    far = down(3)
    far_sum = (down(2).astype(jnp.float32) + across_core(far).astype(jnp.float32)).astype(jnp.bfloat16)
    from_far = across_chip(far_sum)
    activated, far_sum = lax.optimization_barrier((activated, far_sum))
    near = down(1)
    own_mixed = lax.dynamic_slice_in_dim(mixed, rank * width, width, 1)
    near_sum = own_mixed + down(0).astype(jnp.float32) + across_core(near).astype(jnp.float32)
    return ((near_sum + from_far.astype(jnp.float32)).astype(jnp.bfloat16), cache_rows)


def solution(mesh):
    placed = (
        P("req", "tp"),
        P(),
        P("req", None),
        P("req", None),
        P("req", None, None, None),
        P(),
        P(None, "tp"),
        P(),
        P(),
        P(),
        P("tp", None),
        P(),
        P(None, None, "tp"),
        P("tp", None),
    )
    return jax.shard_map(
        functools.partial(local, mesh.shape["req"]),
        mesh=mesh,
        in_specs=placed,
        out_specs=(P("req", "tp"), P("req", None, None)),
        check_vma=False,
    )
```

```python
import functools

import jax
import jax.numpy as jnp
from jax import lax
from jax.experimental import pallas as pl
from jax.experimental.pallas import tpu as pltpu
from jax.sharding import PartitionSpec as P

HEAD_SIZE = 64
PREFIX = 1536

eps_norm = 1e-06
rope_base = 10000.0
masked_score = -1e30
VMEM_LIMIT = 60 * 1024 * 1024


def rms_scale(values, gain_vec):
    mean_sq = jnp.mean(values * values, axis=-1, keepdims=True)
    return values * lax.rsqrt(mean_sq + eps_norm) * gain_vec


def turns(positions, half_size):
    frequency = rope_base ** (-jnp.arange(half_size, dtype=jnp.float32) * 2.0 / (2 * half_size))
    angles = positions.astype(jnp.float32)[:, None] * frequency[None, :]
    return jnp.cos(angles), jnp.sin(angles)


def rotate(values, cos_part, sin_part):
    half_size = values.shape[-1] // 2
    cos_part = cos_part[:, None, :]
    sin_part = sin_part[:, None, :]
    front_half = values[..., :half_size]
    back_half = values[..., half_size:]
    return jnp.concatenate(
        [
            front_half * cos_part - back_half * sin_part,
            back_half * cos_part + front_half * sin_part,
        ],
        axis=-1,
    )


def tn_dot(lhs, rhs):
    return lax.dot_general(lhs, rhs, (((0,), (0,)), ((), ())), preferred_element_type=jnp.float32)


def nn_dot(lhs, rhs):
    return lax.dot_general(lhs, rhs, (((1,), (0,)), ((), ())), preferred_element_type=jnp.float32)


def norm_kernel(rank_ref, own_ref, core_ref, chip_ref, both_ref, gain_ref, full_ref, normed_ref):
    rank = rank_ref[0]
    width = own_ref.shape[1]
    pieces = [own_ref, core_ref, chip_ref, both_ref]
    values = [piece[...].astype(jnp.float32) for piece in pieces]
    total = sum(jnp.sum(v * v, axis=-1, keepdims=True) for v in values)
    scale = lax.rsqrt(total / full_ref.shape[1] + eps_norm)
    for flip, (piece, value) in enumerate(zip(pieces, values)):
        place = pl.multiple_of((rank ^ flip) * width, width)
        columns = pl.ds(place, width)
        full_ref[:, columns] = piece[...]
        normed_ref[:, columns] = (value * scale * gain_ref[:, columns]).astype(jnp.bfloat16)


def gather_norm(rank, pieces, gain):
    rows, width = pieces[0].shape
    block = 128
    full = width * len(pieces)
    piece_spec = pl.BlockSpec((block, width), lambda i, s: (i, 0))
    full_spec = pl.BlockSpec((block, full), lambda i, s: (i, 0))
    return pl.pallas_call(
        norm_kernel,
        out_shape=(
            jax.ShapeDtypeStruct((rows, full), jnp.bfloat16),
            jax.ShapeDtypeStruct((rows, full), jnp.bfloat16),
        ),
        grid_spec=pltpu.PrefetchScalarGridSpec(
            num_scalar_prefetch=1,
            grid=(rows // block,),
            in_specs=[piece_spec] * 4 + [pl.BlockSpec((1, full), lambda i, s: (0, 0))],
            out_specs=[full_spec, full_spec],
        ),
        name="gather_norm",
    )(rank.reshape(1), *pieces, gain.reshape(1, full))


def suffix_kernel(len_ref, q_ref, k_ref, v_ref, out_ref, lse_ref):
    first_len = len_ref[0, 0]
    rows = q_ref.shape[1]
    block = 256
    heads = q_ref.shape[0] // HEAD_SIZE
    for start in range(0, rows, block):
        keys = start + block
        key_index = lax.broadcasted_iota(jnp.int32, (keys, block), 0)
        row_index = lax.broadcasted_iota(jnp.int32, (keys, block), 1) + start
        begin = jnp.where(row_index >= first_len, first_len, 0)
        allowed = (key_index <= row_index) & (key_index >= begin)
        for head in range(heads):
            band = pl.ds(head * HEAD_SIZE, HEAD_SIZE)
            scores = tn_dot(k_ref[band, :keys], q_ref[band, start : start + block])
            scores = jnp.where(allowed, scores, masked_score)
            row_max = jnp.max(scores, axis=0, keepdims=True)
            weights = jnp.exp(scores - row_max)
            total = jnp.sum(weights, axis=0, keepdims=True)
            blended = nn_dot(v_ref[band, :keys], weights.astype(jnp.bfloat16))
            out_ref[band, start : start + block] = blended / total
            lse_ref[head : head + 1, start : start + block] = row_max + jnp.log(total)


def suffix_attend(lengths, q_t, k_t, v_t):
    columns, rows = q_t.shape
    vmem = pl.BlockSpec(memory_space=pltpu.VMEM)
    return pl.pallas_call(
        suffix_kernel,
        out_shape=(
            jax.ShapeDtypeStruct((columns, rows), jnp.float32),
            jax.ShapeDtypeStruct((8, rows), jnp.float32),
        ),
        in_specs=[pl.BlockSpec(memory_space=pltpu.SMEM), vmem, vmem, vmem],
        out_specs=[vmem, vmem],
        cost_estimate=pl.CostEstimate(flops=4 * columns * rows * rows, bytes_accessed=3 << 20, transcendentals=5 * rows * rows),
        name="suffix_attend",
    )(lengths, q_t, k_t, v_t)


def fold(values, op):
    return op(values.reshape(values.shape[0] // 8, 8, values.shape[1]), axis=0)


def turn(place, length):
    return jnp.where(place % 2 == 0, place // 2, length - (place + 1) // 2)


def prefix_kernel(block, chunk, n_units, owners_ref, groups_ref, lengths_ref, me_ref, own_q_ref, other_q_ref, *refs):
    units, last_keys, last_values = refs[: n_units - 1], refs[n_units - 1], refs[n_units]
    (own_out, own_lse, other_out), scratch = refs[n_units + 1 : n_units + 4], refs[n_units + 4 :]
    kv, q_buf, o_buf, l_buf, s_a, s_b, m_a, m_b, sems = scratch
    first_len = lengths_ref[0, 0]
    me = me_ref[0]
    length = n_units // 2
    share = units[0].shape[2]

    def landing(job, kind=slice(None)):
        return kv.at[job // 2, kind, :, pl.ds((job % 2) * share, share)]

    for job in range(4):
        holder = owners_ref[2 * groups_ref[0, job // 2] + job % 2]
        away = turn(me // 2, length) - turn(holder // 2, length)
        away = jnp.where(away < 0, away + length, away)
        wanted = 2 * away + jnp.where(holder % 2 == me % 2, 0, 1)
        for unit in range(n_units - 1):

            @pl.when(wanted == unit)
            def _():
                pltpu.make_async_copy(units[unit], landing(job), sems.at[job]).start()

        @pl.when(wanted == n_units - 1)
        def _():
            pltpu.make_async_copy(last_keys, landing(job, pl.ds(0, 1)), sems.at[job]).start()
            pltpu.make_async_copy(last_values, landing(job, pl.ds(1, 1)), sems.at[job]).start()

    columns, rows = own_out.shape
    q_buf[:columns] = own_q_ref[...]
    q_buf[columns:] = other_q_ref[...]
    for job in range(4):
        pltpu.make_async_copy(units[0], landing(job), sems.at[job]).wait()

    heads = columns // HEAD_SIZE
    per = 2 * heads
    keys = 2 * share
    parts = rows // block
    inside = jnp.clip(first_len, 0, rows)
    n_first = (inside + block - 1) // block
    skipped = inside // block
    pairs = n_first + parts - skipped

    def place(task):
        pair = task // per
        head = task % per
        second = (pair >= n_first).astype(jnp.int32)
        part = jnp.where(second == 1, pair - n_first + skipped, pair)
        cols = pl.ds(pl.multiple_of(part * block, block), block)
        q_band = pl.ds(pl.multiple_of(head * HEAD_SIZE, HEAD_SIZE), HEAD_SIZE)
        k_band = pl.ds(pl.multiple_of((head % heads) * HEAD_SIZE, HEAD_SIZE), HEAD_SIZE)
        return second, part, cols, q_band, k_band, head

    def step(now, later, s_now, m_now, s_later, m_later):
        if now is not None:
            second, part, cols, q_band, k_band, head = place(now)
            peak = m_now[...]
        later_second, _, later_cols, later_q, later_k, _ = place(later)
        query = q_buf[later_q, later_cols]
        top = total = blended = None
        for start in range(0, keys, chunk):
            span = pl.ds(start, chunk)
            scores = tn_dot(kv[later_second, 0, later_k, span], query)
            s_later[span, :] = scores
            folded = fold(scores, jnp.max)
            top = folded if top is None else jnp.maximum(top, folded)
            if now is not None:
                weights = jnp.exp(s_now[span, :] - peak)
                folded = fold(weights, jnp.sum)
                total = folded if total is None else total + folded
                out = nn_dot(kv[second, 1, k_band, span], weights.astype(jnp.bfloat16))
                blended = out if blended is None else blended + out
        m_later[...] = jnp.max(top, axis=0, keepdims=True)
        if now is not None:
            total = jnp.sum(total, axis=0, keepdims=True)
            lane = lax.broadcasted_iota(jnp.int32, (1, block), 1) + part * block
            mine = (lane >= first_len).astype(jnp.int32) == second
            o_buf[q_band, cols] = jnp.where(mine, blended * (1.0 / total), o_buf[q_band, cols])
            l_buf[head, :, cols] = jnp.where(mine, peak + jnp.log(total), l_buf[head, :, cols])

    step(None, 0, None, None, s_a, m_a)

    def two(index, carry):
        task = 2 * index
        step(task, task + 1, s_a, m_a, s_b, m_b)
        step(task + 1, jnp.minimum(task + 2, pairs * per - 1), s_b, m_b, s_a, m_a)
        return carry

    lax.fori_loop(0, pairs * heads, two, 0)
    own_out[...] = o_buf[:columns]
    other_out[:columns] = o_buf[columns:].astype(jnp.bfloat16)
    for head in range(heads):
        own_lse[head : head + 1] = l_buf[head]
    rest = jnp.concatenate([l_buf[heads + head] for head in range(heads)] + [jnp.zeros((8 - heads, rows), jnp.float32)])
    terms = []
    for _ in range(3):
        terms.append(rest.astype(jnp.bfloat16).astype(jnp.float32))
        rest = rest - terms[-1]
    terms.append(jnp.zeros_like(rest))
    other_out[columns:] = jnp.concatenate(terms).astype(jnp.bfloat16)


def prefix_attend(owners, groups, lengths, me, own_q, other_q, units):
    columns, rows = own_q.shape
    share = units[0].shape[2]
    block = 256
    vmem = pl.BlockSpec(memory_space=pltpu.VMEM)
    out = jax.ShapeDtypeStruct((columns, rows), jnp.float32)
    lse = jax.ShapeDtypeStruct((8, rows), jnp.float32)
    sent = jax.ShapeDtypeStruct((columns + 32, rows), jnp.bfloat16)
    return pl.pallas_call(
        functools.partial(prefix_kernel, block, 256, len(units) - 1),
        out_shape=(out, lse, sent),
        in_specs=[pl.BlockSpec(memory_space=pltpu.SMEM)] * 4
        + [vmem] * 2
        + [pl.BlockSpec(memory_space=pl.ANY)] * len(units),
        out_specs=[vmem] * 3,
        scratch_shapes=[
            pltpu.VMEM((2, 2, columns, 2 * share), jnp.bfloat16),
            pltpu.VMEM((2 * columns, rows), jnp.bfloat16),
            pltpu.VMEM((2 * columns, rows), jnp.float32),
            pltpu.VMEM((16, 1, rows), jnp.float32),
            pltpu.VMEM((2 * share, block), jnp.float32),
            pltpu.VMEM((2 * share, block), jnp.float32),
            pltpu.VMEM((1, block), jnp.float32),
            pltpu.VMEM((1, block), jnp.float32),
            pltpu.SemaphoreType.DMA((4,)),
        ],
        cost_estimate=pl.CostEstimate(
            flops=32 * columns * rows * share, bytes_accessed=6 << 20, transcendentals=20 * rows * share
        ),
        name="prefix_attend",
    )(owners, groups, lengths, me, own_q, other_q, *units)


def merge_kernel(own_ref, own_lse_ref, got_ref, suffix_ref, suffix_lse_ref, out_ref):
    columns = own_ref.shape[0]
    packed = got_ref[columns:].astype(jnp.float32)
    got_lse = packed[:8] + packed[8:16] + packed[16:24]
    lses = [own_lse_ref[...], got_lse, suffix_lse_ref[...]]
    for head in range(columns // HEAD_SIZE):
        band = pl.ds(head * HEAD_SIZE, HEAD_SIZE)
        parts = [lse[head : head + 1] for lse in lses]
        top = jnp.maximum(jnp.maximum(parts[0], parts[1]), parts[2])
        factors = [jnp.exp(part - top) for part in parts]
        share = 1.0 / (factors[0] + factors[1] + factors[2])
        out_ref[band] = (
            own_ref[band] * (factors[0] * share)
            + got_ref[band].astype(jnp.float32) * (factors[1] * share)
            + suffix_ref[band] * (factors[2] * share)
        ).astype(jnp.bfloat16)


def merge(own, own_lse, got, suffix, suffix_lse):
    columns, rows = own.shape
    return pl.pallas_call(
        merge_kernel,
        out_shape=jax.ShapeDtypeStruct((columns, rows), jnp.bfloat16),
        grid=(rows // 256,),
        in_specs=[
            pl.BlockSpec((columns, 256), lambda i: (0, i)),
            pl.BlockSpec((8, 256), lambda i: (0, i)),
            pl.BlockSpec((columns + 32, 256), lambda i: (0, i)),
            pl.BlockSpec((columns, 256), lambda i: (0, i)),
            pl.BlockSpec((8, 256), lambda i: (0, i)),
        ],
        out_specs=pl.BlockSpec((columns, 256), lambda i: (0, i)),
        cost_estimate=pl.CostEstimate(flops=8 * columns * rows, bytes_accessed=1 << 20, transcendentals=15 * rows),
        name="merge",
    )(own, own_lse, got, suffix, suffix_lse)


def local(
    n_req,
    tokens,
    owners,
    request_groups,
    request_lengths,
    prefix_cache,
    attn_gain,
    query_weight,
    key_value_weight,
    query_gain,
    key_gain,
    w_out,
    ffn_gain,
    w_gate_up,
    w_down,
):
    row_count, width = tokens.shape
    columns = query_weight.shape[1]
    head_count = columns // HEAD_SIZE
    rank = lax.axis_index("tp")
    my_req = lax.axis_index("req")
    core = rank % 2

    def across_chip(value):
        return lax.ppermute(value, "tp", [(i, i ^ 2) for i in range(4)])

    def across_core(value):
        return lax.ppermute(value, "tp", [(i, i ^ 1) for i in range(4)])

    row_index = jnp.arange(row_count, dtype=jnp.int32)
    first_len = request_lengths[0, 0]
    segment = (row_index >= first_len).astype(jnp.int32)
    position = row_index - segment * first_len + PREFIX
    cos_part, sin_part = turns(position, HEAD_SIZE // 2)

    length = n_req // 2
    share = prefix_cache.shape[2] // 2
    mine = lax.dynamic_slice(jnp.transpose(prefix_cache[0], (0, 2, 1)), (0, 0, core * share), (2, columns, share))

    def ring(value):
        order = [*range(0, length, 2), *range(length - 1 - length % 2, 0, -2)]
        steps = zip(order, order[1:] + order[:1])
        return lax.ppermute(value, "req", [(2 * a + b, 2 * c + b) for a, c in steps for b in range(2)])

    def aside(value):
        return lax.ppermute(value, "req", [(r, r ^ 1) for r in range(n_req)])

    held = [mine, ring(mine)]
    units = [mine, aside(mine)]
    from_chip = across_chip(tokens)
    from_core = across_core(tokens)
    down_blocks = [
        lax.dynamic_slice_in_dim(w_down, (rank ^ flip) * width, width, 1) for flip in range(4)
    ]
    from_chip, down_blocks, cos_part, sin_part = lax.optimization_barrier(
        (from_chip, down_blocks, cos_part, sin_part)
    )
    from_both = across_core(from_chip)
    held[1], _ = lax.optimization_barrier((held[1], from_chip))
    pieces, units[1], _ = lax.optimization_barrier(
        ((tokens, from_core, from_chip, from_both), units[1], held[1])
    )
    full_rows, normalized_input = gather_norm(rank, pieces, attn_gain)

    w_out_held, _ = lax.optimization_barrier((w_out, from_chip))
    w_out_chip = across_chip(w_out_held)
    w_out_core = across_core(w_out)
    w_out_both = across_core(w_out_chip)

    query_rows = jnp.dot(
        normalized_input, query_weight, preferred_element_type=jnp.float32
    ).reshape(row_count, head_count, HEAD_SIZE)
    key_value_rows = jnp.dot(
        normalized_input, key_value_weight, preferred_element_type=jnp.float32
    ).reshape(row_count, 2, head_count, HEAD_SIZE)
    query_rows, key_value_rows, second = lax.optimization_barrier((query_rows, key_value_rows, ring(held[1])))
    units += [held[1], aside(held[1])]
    held.append(second)
    for _ in range(3, length):
        units += [held[-1], aside(held[-1])]
        held.append(ring(held[-1]))
    query_rows = rotate(rms_scale(query_rows, query_gain), cos_part, sin_part).astype(jnp.bfloat16)
    key_rows = rotate(rms_scale(key_value_rows[:, 0], key_gain), cos_part, sin_part).astype(jnp.bfloat16)
    value_rows = key_value_rows[:, 1].astype(jnp.bfloat16)
    cache_rows = jnp.stack(
        [key_rows.reshape(row_count, columns), value_rows.reshape(row_count, columns)],
        axis=1,
    )
    own_q = (query_rows * HEAD_SIZE**-0.5).reshape(row_count, columns).T
    other_q = across_core(own_q)
    suffix_out, suffix_lse = suffix_attend(
        request_lengths, own_q, key_rows.reshape(row_count, columns).T, value_rows.reshape(row_count, columns).T
    )

    held[-1], suffix_out, suffix_lse = lax.optimization_barrier((held[-1], suffix_out, suffix_lse))
    units += [held[-1], aside(held[-1][:1]), ring(units[-1][1:])]
    own_out, own_lse, sent = prefix_attend(
        owners, request_groups, request_lengths, my_req.reshape(1), own_q, other_q, units
    )
    attention = merge(own_out, own_lse, across_core(sent), suffix_out, suffix_lse)
    att_chip = across_chip(attention)
    att_core = across_core(attention)
    near_total = full_rows.astype(jnp.float32) + tn_dot(attention, w_out) + tn_dot(att_core, w_out_core)
    near_total, att_chip = lax.optimization_barrier((near_total, att_chip))
    att_both = across_core(att_chip)
    mixed = near_total + tn_dot(att_chip, w_out_chip) + tn_dot(att_both, w_out_both)
    normed_ffn = rms_scale(mixed, ffn_gain).astype(jnp.bfloat16)
    gate_up = jnp.einsum("rd,dgf->rgf", normed_ffn, w_gate_up, preferred_element_type=jnp.float32)
    activated = (jax.nn.silu(gate_up[:, 0]) * gate_up[:, 1]).astype(jnp.bfloat16)

    def down(flip):
        return jnp.dot(activated, down_blocks[flip], preferred_element_type=jnp.float32).astype(jnp.bfloat16)

    got_far, near = lax.optimization_barrier((across_core(down(3)), down(1)))
    far_sum = (down(2).astype(jnp.float32) + got_far.astype(jnp.float32)).astype(jnp.bfloat16)
    from_far = across_chip(far_sum)
    activated, far_sum = lax.optimization_barrier((activated, far_sum))
    own_mixed = lax.dynamic_slice_in_dim(mixed, rank * width, width, 1)
    near_sum = own_mixed + down(0).astype(jnp.float32) + across_core(near).astype(jnp.float32)
    return ((near_sum + from_far.astype(jnp.float32)).astype(jnp.bfloat16), cache_rows)


def solution(mesh):
    placed = (
        P("req", "tp"),
        P(),
        P("req", None),
        P("req", None),
        P("req", None, None, None),
        P(),
        P(None, "tp"),
        P(),
        P(),
        P(),
        P("tp", None),
        P(),
        P(None, None, "tp"),
        P("tp", None),
    )
    return jax.shard_map(
        functools.partial(local, mesh.shape["req"]),
        mesh=mesh,
        in_specs=placed,
        out_specs=(P("req", "tp"), P("req", None, None)),
        check_vma=False,
    )
```

```python
import functools

import jax
import jax.numpy as jnp
from jax import lax
from jax.experimental import pallas as pl
from jax.experimental.pallas import tpu as pltpu
from jax.sharding import PartitionSpec as P

HEAD_SIZE = 64
PREFIX = 1536

eps_norm = 1e-06
rope_base = 10000.0
masked_score = -1e30
VMEM_LIMIT = 60 * 1024 * 1024


def rms_scale(values, gain_vec):
    mean_sq = jnp.mean(values * values, axis=-1, keepdims=True)
    return values * lax.rsqrt(mean_sq + eps_norm) * gain_vec


def turns(positions, half_size):
    frequency = rope_base ** (-jnp.arange(half_size, dtype=jnp.float32) * 2.0 / (2 * half_size))
    angles = positions.astype(jnp.float32)[:, None] * frequency[None, :]
    return jnp.cos(angles), jnp.sin(angles)


def rotate(values, cos_part, sin_part):
    half_size = values.shape[-1] // 2
    cos_part = cos_part[:, None, :]
    sin_part = sin_part[:, None, :]
    front_half = values[..., :half_size]
    back_half = values[..., half_size:]
    return jnp.concatenate(
        [
            front_half * cos_part - back_half * sin_part,
            back_half * cos_part + front_half * sin_part,
        ],
        axis=-1,
    )


def tn_dot(lhs, rhs):
    return lax.dot_general(lhs, rhs, (((0,), (0,)), ((), ())), preferred_element_type=jnp.float32)


def nn_dot(lhs, rhs):
    return lax.dot_general(lhs, rhs, (((1,), (0,)), ((), ())), preferred_element_type=jnp.float32)


def norm_kernel(rank_ref, own_ref, core_ref, chip_ref, both_ref, gain_ref, full_ref, normed_ref):
    rank = rank_ref[0]
    width = own_ref.shape[1]
    pieces = [own_ref, core_ref, chip_ref, both_ref]
    values = [piece[...].astype(jnp.float32) for piece in pieces]
    total = sum(jnp.sum(v * v, axis=-1, keepdims=True) for v in values)
    scale = lax.rsqrt(total / full_ref.shape[1] + eps_norm)
    for flip, (piece, value) in enumerate(zip(pieces, values)):
        place = pl.multiple_of((rank ^ flip) * width, width)
        columns = pl.ds(place, width)
        full_ref[:, columns] = piece[...]
        normed_ref[:, columns] = (value * scale * gain_ref[:, columns]).astype(jnp.bfloat16)


def gather_norm(rank, pieces, gain):
    rows, width = pieces[0].shape
    block = 128
    full = width * len(pieces)
    piece_spec = pl.BlockSpec((block, width), lambda i, s: (i, 0))
    full_spec = pl.BlockSpec((block, full), lambda i, s: (i, 0))
    return pl.pallas_call(
        norm_kernel,
        out_shape=(
            jax.ShapeDtypeStruct((rows, full), jnp.bfloat16),
            jax.ShapeDtypeStruct((rows, full), jnp.bfloat16),
        ),
        grid_spec=pltpu.PrefetchScalarGridSpec(
            num_scalar_prefetch=1,
            grid=(rows // block,),
            in_specs=[piece_spec] * 4 + [pl.BlockSpec((1, full), lambda i, s: (0, 0))],
            out_specs=[full_spec, full_spec],
        ),
        name="gather_norm",
    )(rank.reshape(1), *pieces, gain.reshape(1, full))


def suffix_kernel(len_ref, q_ref, k_ref, v_ref, out_ref, lse_ref):
    first_len = len_ref[0, 0]
    rows = q_ref.shape[1]
    block = 256
    heads = q_ref.shape[0] // HEAD_SIZE
    for start in range(0, rows, block):
        keys = start + block
        key_index = lax.broadcasted_iota(jnp.int32, (keys, block), 0)
        row_index = lax.broadcasted_iota(jnp.int32, (keys, block), 1) + start
        begin = jnp.where(row_index >= first_len, first_len, 0)
        allowed = (key_index <= row_index) & (key_index >= begin)
        for head in range(heads):
            band = pl.ds(head * HEAD_SIZE, HEAD_SIZE)
            scores = tn_dot(k_ref[band, :keys], q_ref[band, start : start + block])
            scores = jnp.where(allowed, scores, masked_score)
            row_max = jnp.max(scores, axis=0, keepdims=True)
            weights = jnp.exp(scores - row_max)
            total = jnp.sum(weights, axis=0, keepdims=True)
            blended = nn_dot(v_ref[band, :keys], weights.astype(jnp.bfloat16))
            out_ref[band, start : start + block] = blended / total
            lse_ref[head : head + 1, start : start + block] = row_max + jnp.log(total)


def suffix_attend(lengths, q_t, k_t, v_t):
    columns, rows = q_t.shape
    vmem = pl.BlockSpec(memory_space=pltpu.VMEM)
    return pl.pallas_call(
        suffix_kernel,
        out_shape=(
            jax.ShapeDtypeStruct((columns, rows), jnp.float32),
            jax.ShapeDtypeStruct((8, rows), jnp.float32),
        ),
        in_specs=[pl.BlockSpec(memory_space=pltpu.SMEM), vmem, vmem, vmem],
        out_specs=[vmem, vmem],
        cost_estimate=pl.CostEstimate(flops=4 * columns * rows * rows, bytes_accessed=3 << 20, transcendentals=5 * rows * rows),
        name="suffix_attend",
    )(lengths, q_t, k_t, v_t)


def fold(values, op):
    return op(values.reshape(values.shape[0] // 8, 8, values.shape[1]), axis=0)


def turn(place, length):
    return jnp.where(place % 2 == 0, place // 2, length - (place + 1) // 2)


def prefix_kernel(block, chunk, n_units, owners_ref, groups_ref, lengths_ref, me_ref, own_q_ref, other_q_ref, *refs):
    units, last_keys, last_values = refs[: n_units - 1], refs[n_units - 1], refs[n_units]
    (own_out, own_lse, other_out), scratch = refs[n_units + 1 : n_units + 4], refs[n_units + 4 :]
    kv, q_buf, o_buf, l_buf, s_a, s_b, m_a, m_b, sems = scratch
    first_len = lengths_ref[0, 0]
    me = me_ref[0]
    length = n_units // 2
    share = units[0].shape[2]

    def landing(job, kind=slice(None)):
        return kv.at[job // 2, kind, :, pl.ds((job % 2) * share, share)]

    for job in range(4):
        holder = owners_ref[2 * groups_ref[0, job // 2] + job % 2]
        away = turn(me // 2, length) - turn(holder // 2, length)
        away = jnp.where(away < 0, away + length, away)
        wanted = 2 * away + jnp.where(holder % 2 == me % 2, 0, 1)
        for unit in range(n_units - 1):

            @pl.when(wanted == unit)
            def _():
                pltpu.make_async_copy(units[unit], landing(job), sems.at[job]).start()

        @pl.when(wanted == n_units - 1)
        def _():
            pltpu.make_async_copy(last_keys, landing(job, pl.ds(0, 1)), sems.at[job]).start()
            pltpu.make_async_copy(last_values, landing(job, pl.ds(1, 1)), sems.at[job]).start()

    columns, rows = own_out.shape
    q_buf[:columns] = own_q_ref[...]
    q_buf[columns:] = other_q_ref[...]
    for job in range(4):
        pltpu.make_async_copy(units[0], landing(job), sems.at[job]).wait()

    heads = columns // HEAD_SIZE
    per = 2 * heads
    keys = 2 * share
    parts = rows // block
    inside = jnp.clip(first_len, 0, rows)
    n_first = (inside + block - 1) // block
    skipped = inside // block
    pairs = n_first + parts - skipped

    def place(task):
        pair = task // per
        head = task % per
        second = (pair >= n_first).astype(jnp.int32)
        part = jnp.where(second == 1, pair - n_first + skipped, pair)
        cols = pl.ds(pl.multiple_of(part * block, block), block)
        q_band = pl.ds(pl.multiple_of(head * HEAD_SIZE, HEAD_SIZE), HEAD_SIZE)
        k_band = pl.ds(pl.multiple_of((head % heads) * HEAD_SIZE, HEAD_SIZE), HEAD_SIZE)
        return second, part, cols, q_band, k_band, head

    def step(now, later, s_now, m_now, s_later, m_later):
        if now is not None:
            second, part, cols, q_band, k_band, head = place(now)
            peak = m_now[...]
        later_second, _, later_cols, later_q, later_k, _ = place(later)
        query = q_buf[later_q, later_cols]
        top = total = blended = None
        for start in range(0, keys, chunk):
            span = pl.ds(start, chunk)
            scores = tn_dot(kv[later_second, 0, later_k, span], query)
            s_later[span, :] = scores
            folded = fold(scores, jnp.max)
            top = folded if top is None else jnp.maximum(top, folded)
            if now is not None:
                weights = jnp.exp(s_now[span, :] - peak)
                folded = fold(weights, jnp.sum)
                total = folded if total is None else total + folded
                out = nn_dot(kv[second, 1, k_band, span], weights.astype(jnp.bfloat16))
                blended = out if blended is None else blended + out
        m_later[...] = jnp.max(top, axis=0, keepdims=True)
        if now is not None:
            total = jnp.sum(total, axis=0, keepdims=True)
            lane = lax.broadcasted_iota(jnp.int32, (1, block), 1) + part * block
            mine = (lane >= first_len).astype(jnp.int32) == second
            o_buf[q_band, cols] = jnp.where(mine, blended * (1.0 / total), o_buf[q_band, cols])
            l_buf[head, :, cols] = jnp.where(mine, peak + jnp.log(total), l_buf[head, :, cols])

    step(None, 0, None, None, s_a, m_a)

    def two(index, carry):
        task = 2 * index
        step(task, task + 1, s_a, m_a, s_b, m_b)
        step(task + 1, jnp.minimum(task + 2, pairs * per - 1), s_b, m_b, s_a, m_a)
        return carry

    lax.fori_loop(0, pairs * heads, two, 0)
    own_out[...] = o_buf[:columns]
    other_out[:columns] = o_buf[columns:].astype(jnp.bfloat16)
    for head in range(heads):
        own_lse[head : head + 1] = l_buf[head]
    rest = jnp.concatenate([l_buf[heads + head] for head in range(heads)] + [jnp.zeros((8 - heads, rows), jnp.float32)])
    terms = []
    for _ in range(3):
        terms.append(rest.astype(jnp.bfloat16).astype(jnp.float32))
        rest = rest - terms[-1]
    terms.append(jnp.zeros_like(rest))
    other_out[columns:] = jnp.concatenate(terms).astype(jnp.bfloat16)


def prefix_attend(owners, groups, lengths, me, own_q, other_q, units):
    columns, rows = own_q.shape
    share = units[0].shape[2]
    block = 256
    vmem = pl.BlockSpec(memory_space=pltpu.VMEM)
    out = jax.ShapeDtypeStruct((columns, rows), jnp.float32)
    lse = jax.ShapeDtypeStruct((8, rows), jnp.float32)
    sent = jax.ShapeDtypeStruct((columns + 32, rows), jnp.bfloat16)
    return pl.pallas_call(
        functools.partial(prefix_kernel, block, 256, len(units) - 1),
        out_shape=(out, lse, sent),
        in_specs=[pl.BlockSpec(memory_space=pltpu.SMEM)] * 4
        + [vmem] * 2
        + [pl.BlockSpec(memory_space=pl.ANY)] * len(units),
        out_specs=[vmem] * 3,
        scratch_shapes=[
            pltpu.VMEM((2, 2, columns, 2 * share), jnp.bfloat16),
            pltpu.VMEM((2 * columns, rows), jnp.bfloat16),
            pltpu.VMEM((2 * columns, rows), jnp.float32),
            pltpu.VMEM((16, 1, rows), jnp.float32),
            pltpu.VMEM((2 * share, block), jnp.float32),
            pltpu.VMEM((2 * share, block), jnp.float32),
            pltpu.VMEM((1, block), jnp.float32),
            pltpu.VMEM((1, block), jnp.float32),
            pltpu.SemaphoreType.DMA((4,)),
        ],
        cost_estimate=pl.CostEstimate(
            flops=32 * columns * rows * share, bytes_accessed=6 << 20, transcendentals=20 * rows * share
        ),
        name="prefix_attend",
    )(owners, groups, lengths, me, own_q, other_q, *units)


def merge_kernel(own_ref, own_lse_ref, got_ref, suffix_ref, suffix_lse_ref, out_ref):
    columns = own_ref.shape[0]
    packed = got_ref[columns:].astype(jnp.float32)
    got_lse = packed[:8] + packed[8:16] + packed[16:24]
    lses = [own_lse_ref[...], got_lse, suffix_lse_ref[...]]
    for head in range(columns // HEAD_SIZE):
        band = pl.ds(head * HEAD_SIZE, HEAD_SIZE)
        parts = [lse[head : head + 1] for lse in lses]
        top = jnp.maximum(jnp.maximum(parts[0], parts[1]), parts[2])
        factors = [jnp.exp(part - top) for part in parts]
        share = 1.0 / (factors[0] + factors[1] + factors[2])
        out_ref[band] = (
            own_ref[band] * (factors[0] * share)
            + got_ref[band].astype(jnp.float32) * (factors[1] * share)
            + suffix_ref[band] * (factors[2] * share)
        ).astype(jnp.bfloat16)


def merge(own, own_lse, got, suffix, suffix_lse):
    columns, rows = own.shape
    return pl.pallas_call(
        merge_kernel,
        out_shape=jax.ShapeDtypeStruct((columns, rows), jnp.bfloat16),
        grid=(rows // 256,),
        in_specs=[
            pl.BlockSpec((columns, 256), lambda i: (0, i)),
            pl.BlockSpec((8, 256), lambda i: (0, i)),
            pl.BlockSpec((columns + 32, 256), lambda i: (0, i)),
            pl.BlockSpec((columns, 256), lambda i: (0, i)),
            pl.BlockSpec((8, 256), lambda i: (0, i)),
        ],
        out_specs=pl.BlockSpec((columns, 256), lambda i: (0, i)),
        cost_estimate=pl.CostEstimate(flops=8 * columns * rows, bytes_accessed=1 << 20, transcendentals=15 * rows),
        name="merge",
    )(own, own_lse, got, suffix, suffix_lse)


def local(
    n_req,
    tokens,
    owners,
    request_groups,
    request_lengths,
    prefix_cache,
    attn_gain,
    query_weight,
    key_value_weight,
    query_gain,
    key_gain,
    w_out,
    ffn_gain,
    w_gate_up,
    w_down,
):
    row_count, width = tokens.shape
    columns = query_weight.shape[1]
    head_count = columns // HEAD_SIZE
    rank = lax.axis_index("tp")
    my_req = lax.axis_index("req")
    core = rank % 2

    def across_chip(value):
        return lax.ppermute(value, "tp", [(i, i ^ 2) for i in range(4)])

    def across_core(value):
        return lax.ppermute(value, "tp", [(i, i ^ 1) for i in range(4)])

    row_index = jnp.arange(row_count, dtype=jnp.int32)
    first_len = request_lengths[0, 0]
    segment = (row_index >= first_len).astype(jnp.int32)
    position = row_index - segment * first_len + PREFIX
    cos_part, sin_part = turns(position, HEAD_SIZE // 2)

    length = n_req // 2
    share = prefix_cache.shape[2] // 2
    mine = lax.dynamic_slice(jnp.transpose(prefix_cache[0], (0, 2, 1)), (0, 0, core * share), (2, columns, share))

    def ring(value):
        order = [*range(0, length, 2), *range(length - 1 - length % 2, 0, -2)]
        steps = zip(order, order[1:] + order[:1])
        return lax.ppermute(value, "req", [(2 * a + b, 2 * c + b) for a, c in steps for b in range(2)])

    def aside(value):
        return lax.ppermute(value, "req", [(r, r ^ 1) for r in range(n_req)])

    held = [mine, ring(mine)]
    units = [mine, aside(mine)]
    from_chip = across_chip(tokens)
    from_core = across_core(tokens)
    held[1], cos_part, sin_part = lax.optimization_barrier((held[1], cos_part, sin_part))
    from_chip, units[1], _ = lax.optimization_barrier((from_chip, units[1], held[1]))
    from_both = across_core(from_chip)
    full_rows, normalized_input = gather_norm(rank, (tokens, from_core, from_chip, from_both), attn_gain)

    w_out_held, _ = lax.optimization_barrier((w_out, from_chip))
    w_out_chip = across_chip(w_out_held)
    w_out_both = across_core(w_out_chip)

    query_rows = jnp.dot(
        normalized_input, query_weight, preferred_element_type=jnp.float32
    ).reshape(row_count, head_count, HEAD_SIZE)
    key_value_rows = jnp.dot(
        normalized_input, key_value_weight, preferred_element_type=jnp.float32
    ).reshape(row_count, 2, head_count, HEAD_SIZE)
    query_rows, key_value_rows, second = lax.optimization_barrier((query_rows, key_value_rows, ring(held[1])))
    units += [held[1], aside(held[1])]
    held.append(second)
    w_out_held, _ = lax.optimization_barrier((w_out, second))
    w_out_core = across_core(w_out_held)
    for _ in range(3, length):
        units += [held[-1], aside(held[-1])]
        held.append(ring(held[-1]))
    query_rows = rotate(rms_scale(query_rows, query_gain), cos_part, sin_part).astype(jnp.bfloat16)
    key_rows = rotate(rms_scale(key_value_rows[:, 0], key_gain), cos_part, sin_part).astype(jnp.bfloat16)
    value_rows = key_value_rows[:, 1].astype(jnp.bfloat16)
    cache_rows = jnp.stack(
        [key_rows.reshape(row_count, columns), value_rows.reshape(row_count, columns)],
        axis=1,
    )
    own_q = (query_rows * HEAD_SIZE**-0.5).reshape(row_count, columns).T
    other_q = across_core(own_q)
    suffix_out, suffix_lse = suffix_attend(
        request_lengths, own_q, key_rows.reshape(row_count, columns).T, value_rows.reshape(row_count, columns).T
    )

    held[-1], suffix_out, suffix_lse = lax.optimization_barrier((held[-1], suffix_out, suffix_lse))
    units += [held[-1], aside(held[-1][:1]), ring(units[-1][1:])]
    w_down_held, _ = lax.optimization_barrier((w_down, held[-1]))
    down_blocks = [
        lax.dynamic_slice_in_dim(w_down_held, (rank ^ flip) * width, width, 1) for flip in range(4)
    ]
    own_q, down_blocks = lax.optimization_barrier((own_q, down_blocks))
    own_out, own_lse, sent = prefix_attend(
        owners, request_groups, request_lengths, my_req.reshape(1), own_q, other_q, units
    )
    attention = merge(own_out, own_lse, across_core(sent), suffix_out, suffix_lse)
    att_chip = across_chip(attention)
    att_core = across_core(attention)
    near_total = full_rows.astype(jnp.float32) + tn_dot(attention, w_out) + tn_dot(att_core, w_out_core)
    near_total, att_chip = lax.optimization_barrier((near_total, att_chip))
    att_both = across_core(att_chip)
    mixed = near_total + tn_dot(att_chip, w_out_chip) + tn_dot(att_both, w_out_both)
    normed_ffn = rms_scale(mixed, ffn_gain).astype(jnp.bfloat16)
    gate_up = jnp.einsum("rd,dgf->rgf", normed_ffn, w_gate_up, preferred_element_type=jnp.float32)
    activated = (jax.nn.silu(gate_up[:, 0]) * gate_up[:, 1]).astype(jnp.bfloat16)

    def down(flip):
        return jnp.dot(activated, down_blocks[flip], preferred_element_type=jnp.float32).astype(jnp.bfloat16)

    got_far, near = lax.optimization_barrier((across_core(down(3)), down(1)))
    far_sum = (down(2).astype(jnp.float32) + got_far.astype(jnp.float32)).astype(jnp.bfloat16)
    from_far = across_chip(far_sum)
    activated, far_sum = lax.optimization_barrier((activated, far_sum))
    own_mixed = lax.dynamic_slice_in_dim(mixed, rank * width, width, 1)
    near_sum = own_mixed + down(0).astype(jnp.float32) + across_core(near).astype(jnp.float32)
    return ((near_sum + from_far.astype(jnp.float32)).astype(jnp.bfloat16), cache_rows)


def solution(mesh):
    placed = (
        P("req", "tp"),
        P(),
        P("req", None),
        P("req", None),
        P("req", None, None, None),
        P(),
        P(None, "tp"),
        P(),
        P(),
        P(),
        P("tp", None),
        P(),
        P(None, None, "tp"),
        P("tp", None),
    )
    return jax.shard_map(
        functools.partial(local, mesh.shape["req"]),
        mesh=mesh,
        in_specs=placed,
        out_specs=(P("req", "tp"), P("req", None, None)),
        check_vma=False,
    )
```

```python
import functools

import jax
import jax.numpy as jnp
from jax import lax
from jax.experimental import pallas as pl
from jax.experimental.pallas import tpu as pltpu
from jax.sharding import PartitionSpec as P

HEAD_SIZE = 64
PREFIX = 1536

eps_norm = 1e-06
rope_base = 10000.0
masked_score = -1e30
VMEM_LIMIT = 60 * 1024 * 1024


def rms_scale(values, gain_vec):
    mean_sq = jnp.mean(values * values, axis=-1, keepdims=True)
    return values * lax.rsqrt(mean_sq + eps_norm) * gain_vec


def turns(positions, half_size):
    frequency = rope_base ** (-jnp.arange(half_size, dtype=jnp.float32) * 2.0 / (2 * half_size))
    angles = positions.astype(jnp.float32)[:, None] * frequency[None, :]
    return jnp.cos(angles), jnp.sin(angles)


def rotate(values, cos_part, sin_part):
    half_size = values.shape[-1] // 2
    cos_part = cos_part[:, None, :]
    sin_part = sin_part[:, None, :]
    front_half = values[..., :half_size]
    back_half = values[..., half_size:]
    return jnp.concatenate(
        [
            front_half * cos_part - back_half * sin_part,
            back_half * cos_part + front_half * sin_part,
        ],
        axis=-1,
    )


def tn_dot(lhs, rhs):
    return lax.dot_general(lhs, rhs, (((0,), (0,)), ((), ())), preferred_element_type=jnp.float32)


def nn_dot(lhs, rhs):
    return lax.dot_general(lhs, rhs, (((1,), (0,)), ((), ())), preferred_element_type=jnp.float32)


def norm_kernel(rank_ref, own_ref, core_ref, chip_ref, both_ref, gain_ref, full_ref, normed_ref):
    rank = rank_ref[0]
    width = own_ref.shape[1]
    pieces = [own_ref, core_ref, chip_ref, both_ref]
    values = [piece[...].astype(jnp.float32) for piece in pieces]
    total = sum(jnp.sum(v * v, axis=-1, keepdims=True) for v in values)
    scale = lax.rsqrt(total / full_ref.shape[1] + eps_norm)
    for flip, (piece, value) in enumerate(zip(pieces, values)):
        place = pl.multiple_of((rank ^ flip) * width, width)
        columns = pl.ds(place, width)
        full_ref[:, columns] = piece[...]
        normed_ref[:, columns] = (value * scale * gain_ref[:, columns]).astype(jnp.bfloat16)


def gather_norm(rank, pieces, gain):
    rows, width = pieces[0].shape
    block = 128
    full = width * len(pieces)
    piece_spec = pl.BlockSpec((block, width), lambda i, s: (i, 0))
    full_spec = pl.BlockSpec((block, full), lambda i, s: (i, 0))
    return pl.pallas_call(
        norm_kernel,
        out_shape=(
            jax.ShapeDtypeStruct((rows, full), jnp.bfloat16),
            jax.ShapeDtypeStruct((rows, full), jnp.bfloat16),
        ),
        grid_spec=pltpu.PrefetchScalarGridSpec(
            num_scalar_prefetch=1,
            grid=(rows // block,),
            in_specs=[piece_spec] * 4 + [pl.BlockSpec((1, full), lambda i, s: (0, 0))],
            out_specs=[full_spec, full_spec],
        ),
        name="gather_norm",
    )(rank.reshape(1), *pieces, gain.reshape(1, full))


def suffix_kernel(len_ref, q_ref, k_ref, v_ref, out_ref, lse_ref):
    first_len = len_ref[0, 0]
    rows = q_ref.shape[1]
    block = 256
    heads = q_ref.shape[0] // HEAD_SIZE
    for start in range(0, rows, block):
        keys = start + block
        key_index = lax.broadcasted_iota(jnp.int32, (keys, block), 0)
        row_index = lax.broadcasted_iota(jnp.int32, (keys, block), 1) + start
        begin = jnp.where(row_index >= first_len, first_len, 0)
        allowed = (key_index <= row_index) & (key_index >= begin)
        for head in range(heads):
            band = pl.ds(head * HEAD_SIZE, HEAD_SIZE)
            scores = tn_dot(k_ref[band, :keys], q_ref[band, start : start + block])
            scores = jnp.where(allowed, scores, masked_score)
            row_max = jnp.max(scores, axis=0, keepdims=True)
            weights = jnp.exp(scores - row_max)
            total = jnp.sum(weights, axis=0, keepdims=True)
            blended = nn_dot(v_ref[band, :keys], weights.astype(jnp.bfloat16))
            out_ref[band, start : start + block] = blended / total
            lse_ref[head : head + 1, start : start + block] = row_max + jnp.log(total)


def suffix_attend(lengths, q_t, k_t, v_t):
    columns, rows = q_t.shape
    vmem = pl.BlockSpec(memory_space=pltpu.VMEM)
    return pl.pallas_call(
        suffix_kernel,
        out_shape=(
            jax.ShapeDtypeStruct((columns, rows), jnp.float32),
            jax.ShapeDtypeStruct((8, rows), jnp.float32),
        ),
        in_specs=[pl.BlockSpec(memory_space=pltpu.SMEM), vmem, vmem, vmem],
        out_specs=[vmem, vmem],
        cost_estimate=pl.CostEstimate(flops=4 * columns * rows * rows, bytes_accessed=3 << 20, transcendentals=5 * rows * rows),
        name="suffix_attend",
    )(lengths, q_t, k_t, v_t)


def fold(values, op):
    return op(values.reshape(values.shape[0] // 8, 8, values.shape[1]), axis=0)


def turn(place, length):
    return jnp.where(place % 2 == 0, place // 2, length - (place + 1) // 2)


def prefix_kernel(block, chunk, n_units, owners_ref, groups_ref, lengths_ref, me_ref, own_q_ref, other_q_ref, *refs):
    units, last_keys, last_values = refs[: n_units - 1], refs[n_units - 1], refs[n_units]
    (own_out, own_lse, other_out), scratch = refs[n_units + 1 : n_units + 4], refs[n_units + 4 :]
    kv, q_buf, o_buf, l_buf, s_a, s_b, m_a, m_b, sems = scratch
    first_len = lengths_ref[0, 0]
    me = me_ref[0]
    length = n_units // 2
    share = units[0].shape[2]

    def landing(job, kind=slice(None)):
        return kv.at[job // 2, kind, :, pl.ds((job % 2) * share, share)]

    for job in range(4):
        holder = owners_ref[2 * groups_ref[0, job // 2] + job % 2]
        away = turn(me // 2, length) - turn(holder // 2, length)
        away = jnp.where(away < 0, away + length, away)
        wanted = 2 * away + jnp.where(holder % 2 == me % 2, 0, 1)
        for unit in range(n_units - 1):

            @pl.when(wanted == unit)
            def _():
                pltpu.make_async_copy(units[unit], landing(job), sems.at[job]).start()

        @pl.when(wanted == n_units - 1)
        def _():
            pltpu.make_async_copy(last_keys, landing(job, pl.ds(0, 1)), sems.at[job]).start()
            pltpu.make_async_copy(last_values, landing(job, pl.ds(1, 1)), sems.at[job]).start()

    columns, rows = own_out.shape
    q_buf[:columns] = own_q_ref[...]
    q_buf[columns:] = other_q_ref[...]
    for job in range(4):
        pltpu.make_async_copy(units[0], landing(job), sems.at[job]).wait()

    heads = columns // HEAD_SIZE
    per = 2 * heads
    keys = 2 * share
    parts = rows // block
    inside = jnp.clip(first_len, 0, rows)
    n_first = (inside + block - 1) // block
    skipped = inside // block
    pairs = n_first + parts - skipped

    def place(task, head=None):
        pair = task // per
        head = task % per if head is None else head
        second = (pair >= n_first).astype(jnp.int32)
        part = jnp.where(second == 1, pair - n_first + skipped, pair)
        cols = pl.ds(pl.multiple_of(part * block, block), block)
        q_band = pl.ds(pl.multiple_of(head * HEAD_SIZE, HEAD_SIZE), HEAD_SIZE)
        k_band = pl.ds(pl.multiple_of((head % heads) * HEAD_SIZE, HEAD_SIZE), HEAD_SIZE)
        return second, part, cols, q_band, k_band, head

    def step(now, later, s_now, m_now, s_later, m_later):
        if now is not None:
            second, part, cols, q_band, k_band, head = place(now)
            peak = m_now[...]
        later_second, _, later_cols, later_q, later_k, _ = place(later)
        query = q_buf[later_q, later_cols]
        top = total = blended = None
        for start in range(0, keys, chunk):
            span = pl.ds(start, chunk)
            scores = tn_dot(kv[later_second, 0, later_k, span], query)
            s_later[span, :] = scores
            folded = fold(scores, jnp.max)
            top = folded if top is None else jnp.maximum(top, folded)
            if now is not None:
                weights = jnp.exp(s_now[span, :] - peak)
                folded = fold(weights, jnp.sum)
                total = folded if total is None else total + folded
                out = nn_dot(kv[second, 1, k_band, span], weights.astype(jnp.bfloat16))
                blended = out if blended is None else blended + out
        m_later[...] = jnp.max(top, axis=0, keepdims=True)
        if now is not None:
            total = jnp.sum(total, axis=0, keepdims=True)
            lane = lax.broadcasted_iota(jnp.int32, (1, block), 1) + part * block
            mine = (lane >= first_len).astype(jnp.int32) == second
            o_buf[q_band, cols] = jnp.where(mine, blended * (1.0 / total), o_buf[q_band, cols])
            l_buf[head, :, cols] = jnp.where(mine, peak + jnp.log(total), l_buf[head, :, cols])

    def group(pair, outside):
        for head in range(per):
            second, part, cols, q_band, k_band, _ = place(pair * per + head, head)
            query = q_buf[q_band, cols]
            total = blended = None
            for start in range(0, keys, chunk):
                span = pl.ds(start, chunk)
                weights = jnp.exp(tn_dot(kv[second, 0, k_band, span], query))
                folded = fold(weights, jnp.sum)
                total = folded if total is None else total + folded
                out = nn_dot(kv[second, 1, k_band, span], weights.astype(jnp.bfloat16))
                blended = out if blended is None else blended + out
            total = jnp.sum(total, axis=0, keepdims=True)
            lane = lax.broadcasted_iota(jnp.int32, (1, block), 1) + part * block
            mine = (lane >= first_len).astype(jnp.int32) == second
            o_buf[q_band, cols] = jnp.where(mine, blended * (1.0 / total), o_buf[q_band, cols])
            l_buf[head, :, cols] = jnp.where(mine, jnp.log(total), l_buf[head, :, cols])
            inside_range = (total > 1e-20) & (total < 1e20)
            outside = jnp.maximum(outside, jnp.where(inside_range | ~mine, 0.0, 1.0))
        return outside

    outside = lax.fori_loop(0, pairs, group, jnp.zeros((1, block), jnp.float32))

    def two(index, carry):
        task = 2 * index
        step(task, task + 1, s_a, m_a, s_b, m_b)
        step(task + 1, jnp.minimum(task + 2, pairs * per - 1), s_b, m_b, s_a, m_a)
        return carry

    @pl.when(jnp.max(outside) > 0.0)
    def _():
        step(None, 0, None, None, s_a, m_a)
        lax.fori_loop(0, pairs * heads, two, 0)

    own_out[...] = o_buf[:columns]
    other_out[:columns] = o_buf[columns:].astype(jnp.bfloat16)
    for head in range(heads):
        own_lse[head : head + 1] = l_buf[head]
    rest = jnp.concatenate([l_buf[heads + head] for head in range(heads)] + [jnp.zeros((8 - heads, rows), jnp.float32)])
    terms = []
    for _ in range(3):
        terms.append(rest.astype(jnp.bfloat16).astype(jnp.float32))
        rest = rest - terms[-1]
    terms.append(jnp.zeros_like(rest))
    other_out[columns:] = jnp.concatenate(terms).astype(jnp.bfloat16)


def prefix_attend(owners, groups, lengths, me, own_q, other_q, units):
    columns, rows = own_q.shape
    share = units[0].shape[2]
    block = 256
    vmem = pl.BlockSpec(memory_space=pltpu.VMEM)
    out = jax.ShapeDtypeStruct((columns, rows), jnp.float32)
    lse = jax.ShapeDtypeStruct((8, rows), jnp.float32)
    sent = jax.ShapeDtypeStruct((columns + 32, rows), jnp.bfloat16)
    return pl.pallas_call(
        functools.partial(prefix_kernel, block, 256, len(units) - 1),
        out_shape=(out, lse, sent),
        in_specs=[pl.BlockSpec(memory_space=pltpu.SMEM)] * 4
        + [vmem] * 2
        + [pl.BlockSpec(memory_space=pl.ANY)] * len(units),
        out_specs=[vmem] * 3,
        scratch_shapes=[
            pltpu.VMEM((2, 2, columns, 2 * share), jnp.bfloat16),
            pltpu.VMEM((2 * columns, rows), jnp.bfloat16),
            pltpu.VMEM((2 * columns, rows), jnp.float32),
            pltpu.VMEM((16, 1, rows), jnp.float32),
            pltpu.VMEM((2 * share, block), jnp.float32),
            pltpu.VMEM((2 * share, block), jnp.float32),
            pltpu.VMEM((1, block), jnp.float32),
            pltpu.VMEM((1, block), jnp.float32),
            pltpu.SemaphoreType.DMA((4,)),
        ],
        cost_estimate=pl.CostEstimate(
            flops=32 * columns * rows * share, bytes_accessed=6 << 20, transcendentals=20 * rows * share
        ),
        name="prefix_attend",
    )(owners, groups, lengths, me, own_q, other_q, *units)


def merge_kernel(own_ref, own_lse_ref, got_ref, suffix_ref, suffix_lse_ref, out_ref):
    columns = own_ref.shape[0]
    packed = got_ref[columns:].astype(jnp.float32)
    got_lse = packed[:8] + packed[8:16] + packed[16:24]
    lses = [own_lse_ref[...], got_lse, suffix_lse_ref[...]]
    for head in range(columns // HEAD_SIZE):
        band = pl.ds(head * HEAD_SIZE, HEAD_SIZE)
        parts = [lse[head : head + 1] for lse in lses]
        top = jnp.maximum(jnp.maximum(parts[0], parts[1]), parts[2])
        factors = [jnp.exp(part - top) for part in parts]
        share = 1.0 / (factors[0] + factors[1] + factors[2])
        out_ref[band] = (
            own_ref[band] * (factors[0] * share)
            + got_ref[band].astype(jnp.float32) * (factors[1] * share)
            + suffix_ref[band] * (factors[2] * share)
        ).astype(jnp.bfloat16)


def merge(own, own_lse, got, suffix, suffix_lse):
    columns, rows = own.shape
    return pl.pallas_call(
        merge_kernel,
        out_shape=jax.ShapeDtypeStruct((columns, rows), jnp.bfloat16),
        grid=(rows // 256,),
        in_specs=[
            pl.BlockSpec((columns, 256), lambda i: (0, i)),
            pl.BlockSpec((8, 256), lambda i: (0, i)),
            pl.BlockSpec((columns + 32, 256), lambda i: (0, i)),
            pl.BlockSpec((columns, 256), lambda i: (0, i)),
            pl.BlockSpec((8, 256), lambda i: (0, i)),
        ],
        out_specs=pl.BlockSpec((columns, 256), lambda i: (0, i)),
        cost_estimate=pl.CostEstimate(flops=8 * columns * rows, bytes_accessed=1 << 20, transcendentals=15 * rows),
        name="merge",
    )(own, own_lse, got, suffix, suffix_lse)


def local(
    n_req,
    tokens,
    owners,
    request_groups,
    request_lengths,
    prefix_cache,
    attn_gain,
    query_weight,
    key_value_weight,
    query_gain,
    key_gain,
    w_out,
    ffn_gain,
    w_gate_up,
    w_down,
):
    row_count, width = tokens.shape
    columns = query_weight.shape[1]
    head_count = columns // HEAD_SIZE
    rank = lax.axis_index("tp")
    my_req = lax.axis_index("req")
    core = rank % 2

    def across_chip(value):
        return lax.ppermute(value, "tp", [(i, i ^ 2) for i in range(4)])

    def across_core(value):
        return lax.ppermute(value, "tp", [(i, i ^ 1) for i in range(4)])

    row_index = jnp.arange(row_count, dtype=jnp.int32)
    first_len = request_lengths[0, 0]
    segment = (row_index >= first_len).astype(jnp.int32)
    position = row_index - segment * first_len + PREFIX
    cos_part, sin_part = turns(position, HEAD_SIZE // 2)

    length = n_req // 2
    share = prefix_cache.shape[2] // 2
    mine = lax.dynamic_slice(jnp.transpose(prefix_cache[0], (0, 2, 1)), (0, 0, core * share), (2, columns, share))

    def ring(value):
        order = [*range(0, length, 2), *range(length - 1 - length % 2, 0, -2)]
        steps = zip(order, order[1:] + order[:1])
        return lax.ppermute(value, "req", [(2 * a + b, 2 * c + b) for a, c in steps for b in range(2)])

    def aside(value):
        return lax.ppermute(value, "req", [(r, r ^ 1) for r in range(n_req)])

    held = [mine, ring(mine)]
    units = [mine, aside(mine)]
    from_chip = across_chip(tokens)
    from_core = across_core(tokens)
    held[1], cos_part, sin_part = lax.optimization_barrier((held[1], cos_part, sin_part))
    from_chip, units[1], _ = lax.optimization_barrier((from_chip, units[1], held[1]))
    from_both = across_core(from_chip)
    full_rows, normalized_input = gather_norm(rank, (tokens, from_core, from_chip, from_both), attn_gain)

    w_out_held, _ = lax.optimization_barrier((w_out, from_chip))
    w_out_chip = across_chip(w_out_held)
    w_out_both = across_core(w_out_chip)

    query_rows = jnp.dot(
        normalized_input, query_weight, preferred_element_type=jnp.float32
    ).reshape(row_count, head_count, HEAD_SIZE)
    key_value_rows = jnp.dot(
        normalized_input, key_value_weight, preferred_element_type=jnp.float32
    ).reshape(row_count, 2, head_count, HEAD_SIZE)
    query_rows, key_value_rows, second = lax.optimization_barrier((query_rows, key_value_rows, ring(held[1])))
    units += [held[1], aside(held[1])]
    held.append(second)
    w_out_held, _ = lax.optimization_barrier((w_out, second))
    w_out_core = across_core(w_out_held)
    for _ in range(3, length):
        units += [held[-1], aside(held[-1])]
        held.append(ring(held[-1]))
    query_rows = rotate(rms_scale(query_rows, query_gain), cos_part, sin_part).astype(jnp.bfloat16)
    key_rows = rotate(rms_scale(key_value_rows[:, 0], key_gain), cos_part, sin_part).astype(jnp.bfloat16)
    value_rows = key_value_rows[:, 1].astype(jnp.bfloat16)
    cache_rows = jnp.stack(
        [key_rows.reshape(row_count, columns), value_rows.reshape(row_count, columns)],
        axis=1,
    )
    own_q = (query_rows * HEAD_SIZE**-0.5).reshape(row_count, columns).T
    other_q = across_core(own_q)
    suffix_out, suffix_lse = suffix_attend(
        request_lengths, own_q, key_rows.reshape(row_count, columns).T, value_rows.reshape(row_count, columns).T
    )

    held[-1], suffix_out, suffix_lse = lax.optimization_barrier((held[-1], suffix_out, suffix_lse))
    units += [held[-1], aside(held[-1][:1]), ring(units[-1][1:])]
    w_down_held, _ = lax.optimization_barrier((w_down, held[-1]))
    down_blocks = [
        lax.dynamic_slice_in_dim(w_down_held, (rank ^ flip) * width, width, 1) for flip in range(4)
    ]
    own_q, down_blocks = lax.optimization_barrier((own_q, down_blocks))
    own_out, own_lse, sent = prefix_attend(
        owners, request_groups, request_lengths, my_req.reshape(1), own_q, other_q, units
    )
    attention = merge(own_out, own_lse, across_core(sent), suffix_out, suffix_lse)
    att_chip = across_chip(attention)
    att_core = across_core(attention)
    near_total = full_rows.astype(jnp.float32) + tn_dot(attention, w_out) + tn_dot(att_core, w_out_core)
    near_total, att_chip = lax.optimization_barrier((near_total, att_chip))
    att_both = across_core(att_chip)
    mixed = near_total + tn_dot(att_chip, w_out_chip) + tn_dot(att_both, w_out_both)
    normed_ffn = rms_scale(mixed, ffn_gain).astype(jnp.bfloat16)
    gate_up = jnp.einsum("rd,dgf->rgf", normed_ffn, w_gate_up, preferred_element_type=jnp.float32)
    activated = (jax.nn.silu(gate_up[:, 0]) * gate_up[:, 1]).astype(jnp.bfloat16)

    def down(flip):
        return jnp.dot(activated, down_blocks[flip], preferred_element_type=jnp.float32).astype(jnp.bfloat16)

    got_far, near = lax.optimization_barrier((across_core(down(3)), down(1)))
    far_sum = (down(2).astype(jnp.float32) + got_far.astype(jnp.float32)).astype(jnp.bfloat16)
    from_far = across_chip(far_sum)
    activated, far_sum = lax.optimization_barrier((activated, far_sum))
    own_mixed = lax.dynamic_slice_in_dim(mixed, rank * width, width, 1)
    near_sum = own_mixed + down(0).astype(jnp.float32) + across_core(near).astype(jnp.float32)
    return ((near_sum + from_far.astype(jnp.float32)).astype(jnp.bfloat16), cache_rows)


def solution(mesh):
    placed = (
        P("req", "tp"),
        P(),
        P("req", None),
        P("req", None),
        P("req", None, None, None),
        P(),
        P(None, "tp"),
        P(),
        P(),
        P(),
        P("tp", None),
        P(),
        P(None, None, "tp"),
        P("tp", None),
    )
    return jax.shard_map(
        functools.partial(local, mesh.shape["req"]),
        mesh=mesh,
        in_specs=placed,
        out_specs=(P("req", "tp"), P("req", None, None)),
        check_vma=False,
    )
```

```python
import functools

import jax
import jax.numpy as jnp
from jax import lax
from jax.experimental import pallas as pl
from jax.experimental.pallas import tpu as pltpu
from jax.sharding import PartitionSpec as P

HEAD_SIZE = 64
PREFIX = 1536

eps_norm = 1e-06
rope_base = 10000.0
masked_score = -1e30
VMEM_LIMIT = 60 * 1024 * 1024


def rms_scale(values, gain_vec):
    mean_sq = jnp.mean(values * values, axis=-1, keepdims=True)
    return values * lax.rsqrt(mean_sq + eps_norm) * gain_vec


def turns(positions, half_size):
    frequency = rope_base ** (-jnp.arange(half_size, dtype=jnp.float32) * 2.0 / (2 * half_size))
    angles = positions.astype(jnp.float32)[:, None] * frequency[None, :]
    return jnp.cos(angles), jnp.sin(angles)


def rotate(values, cos_part, sin_part):
    half_size = values.shape[-1] // 2
    cos_part = cos_part[:, None, :]
    sin_part = sin_part[:, None, :]
    front_half = values[..., :half_size]
    back_half = values[..., half_size:]
    return jnp.concatenate(
        [
            front_half * cos_part - back_half * sin_part,
            back_half * cos_part + front_half * sin_part,
        ],
        axis=-1,
    )


def tn_dot(lhs, rhs):
    return lax.dot_general(lhs, rhs, (((0,), (0,)), ((), ())), preferred_element_type=jnp.float32)


def nn_dot(lhs, rhs):
    return lax.dot_general(lhs, rhs, (((1,), (0,)), ((), ())), preferred_element_type=jnp.float32)


def norm_kernel(rank_ref, own_ref, core_ref, chip_ref, both_ref, gain_ref, full_ref, normed_ref):
    rank = rank_ref[0]
    width = own_ref.shape[1]
    pieces = [own_ref, core_ref, chip_ref, both_ref]
    values = [piece[...].astype(jnp.float32) for piece in pieces]
    total = sum(jnp.sum(v * v, axis=-1, keepdims=True) for v in values)
    scale = lax.rsqrt(total / full_ref.shape[1] + eps_norm)
    for flip, (piece, value) in enumerate(zip(pieces, values)):
        place = pl.multiple_of((rank ^ flip) * width, width)
        columns = pl.ds(place, width)
        full_ref[:, columns] = piece[...]
        normed_ref[:, columns] = (value * scale * gain_ref[:, columns]).astype(jnp.bfloat16)


def gather_norm(rank, pieces, gain):
    rows, width = pieces[0].shape
    block = 128
    full = width * len(pieces)
    piece_spec = pl.BlockSpec((block, width), lambda i, s: (i, 0))
    full_spec = pl.BlockSpec((block, full), lambda i, s: (i, 0))
    return pl.pallas_call(
        norm_kernel,
        out_shape=(
            jax.ShapeDtypeStruct((rows, full), jnp.bfloat16),
            jax.ShapeDtypeStruct((rows, full), jnp.bfloat16),
        ),
        grid_spec=pltpu.PrefetchScalarGridSpec(
            num_scalar_prefetch=1,
            grid=(rows // block,),
            in_specs=[piece_spec] * 4 + [pl.BlockSpec((1, full), lambda i, s: (0, 0))],
            out_specs=[full_spec, full_spec],
        ),
        name="gather_norm",
    )(rank.reshape(1), *pieces, gain.reshape(1, full))


def suffix_kernel(len_ref, q_ref, k_ref, v_ref, out_ref, lse_ref):
    first_len = len_ref[0, 0]
    rows = q_ref.shape[1]
    block = 256
    heads = q_ref.shape[0] // HEAD_SIZE
    for start in range(0, rows, block):
        keys = start + block
        key_index = lax.broadcasted_iota(jnp.int32, (keys, block), 0)
        row_index = lax.broadcasted_iota(jnp.int32, (keys, block), 1) + start
        begin = jnp.where(row_index >= first_len, first_len, 0)
        allowed = (key_index <= row_index) & (key_index >= begin)
        for head in range(heads):
            band = pl.ds(head * HEAD_SIZE, HEAD_SIZE)
            scores = tn_dot(k_ref[band, :keys], q_ref[band, start : start + block])
            scores = jnp.where(allowed, scores, masked_score)
            row_max = jnp.max(scores, axis=0, keepdims=True)
            weights = jnp.exp(scores - row_max)
            total = jnp.sum(weights, axis=0, keepdims=True)
            blended = nn_dot(v_ref[band, :keys], weights.astype(jnp.bfloat16))
            out_ref[band, start : start + block] = blended / total
            lse_ref[head : head + 1, start : start + block] = row_max + jnp.log(total)


def suffix_attend(lengths, q_t, k_t, v_t):
    columns, rows = q_t.shape
    vmem = pl.BlockSpec(memory_space=pltpu.VMEM)
    return pl.pallas_call(
        suffix_kernel,
        out_shape=(
            jax.ShapeDtypeStruct((columns, rows), jnp.float32),
            jax.ShapeDtypeStruct((8, rows), jnp.float32),
        ),
        in_specs=[pl.BlockSpec(memory_space=pltpu.SMEM), vmem, vmem, vmem],
        out_specs=[vmem, vmem],
        cost_estimate=pl.CostEstimate(flops=4 * columns * rows * rows, bytes_accessed=3 << 20, transcendentals=5 * rows * rows),
        name="suffix_attend",
    )(lengths, q_t, k_t, v_t)


def fold(values, op):
    return op(values.reshape(values.shape[0] // 8, 8, values.shape[1]), axis=0)


def turn(place, length):
    return jnp.where(place % 2 == 0, place // 2, length - (place + 1) // 2)


def prefix_kernel(block, chunk, n_units, owners_ref, groups_ref, lengths_ref, me_ref, own_q_ref, other_q_ref, *refs):
    units, last_keys, last_values = refs[: n_units - 1], refs[n_units - 1], refs[n_units]
    (own_out, own_lse, other_out), scratch = refs[n_units + 1 : n_units + 4], refs[n_units + 4 :]
    kv, q_buf, o_buf, l_buf, s_a, s_b, m_a, m_b, sems = scratch
    first_len = lengths_ref[0, 0]
    me = me_ref[0]
    length = n_units // 2
    share = units[0].shape[2]

    def landing(job, kind=slice(None)):
        return kv.at[job // 2, kind, :, pl.ds((job % 2) * share, share)]

    for job in range(4):
        holder = owners_ref[2 * groups_ref[0, job // 2] + job % 2]
        away = turn(me // 2, length) - turn(holder // 2, length)
        away = jnp.where(away < 0, away + length, away)
        wanted = 2 * away + jnp.where(holder % 2 == me % 2, 0, 1)
        for unit in range(n_units - 1):

            @pl.when(wanted == unit)
            def _():
                pltpu.make_async_copy(units[unit], landing(job), sems.at[job]).start()

        @pl.when(wanted == n_units - 1)
        def _():
            pltpu.make_async_copy(last_keys, landing(job, pl.ds(0, 1)), sems.at[job]).start()
            pltpu.make_async_copy(last_values, landing(job, pl.ds(1, 1)), sems.at[job]).start()

    columns, rows = own_out.shape
    q_buf[:columns] = own_q_ref[...]
    q_buf[columns:] = other_q_ref[...]
    for job in range(4):
        pltpu.make_async_copy(units[0], landing(job), sems.at[job]).wait()

    heads = columns // HEAD_SIZE
    per = 2 * heads
    keys = 2 * share
    parts = rows // block
    inside = jnp.clip(first_len, 0, rows)
    n_first = (inside + block - 1) // block
    skipped = inside // block
    pairs = n_first + parts - skipped

    def place(task, head=None):
        pair = task // per
        head = task % per if head is None else head
        second = (pair >= n_first).astype(jnp.int32)
        part = jnp.where(second == 1, pair - n_first + skipped, pair)
        cols = pl.ds(pl.multiple_of(part * block, block), block)
        q_band = pl.ds(pl.multiple_of(head * HEAD_SIZE, HEAD_SIZE), HEAD_SIZE)
        k_band = pl.ds(pl.multiple_of((head % heads) * HEAD_SIZE, HEAD_SIZE), HEAD_SIZE)
        return second, part, cols, q_band, k_band, head

    def step(now, later, s_now, m_now, s_later, m_later):
        if now is not None:
            second, part, cols, q_band, k_band, head = place(now)
            peak = m_now[...]
        later_second, _, later_cols, later_q, later_k, _ = place(later)
        query = q_buf[later_q, later_cols]
        top = total = blended = None
        for start in range(0, keys, chunk):
            span = pl.ds(start, chunk)
            scores = tn_dot(kv[later_second, 0, later_k, span], query)
            s_later[span, :] = scores
            folded = fold(scores, jnp.max)
            top = folded if top is None else jnp.maximum(top, folded)
            if now is not None:
                weights = jnp.exp(s_now[span, :] - peak)
                folded = fold(weights, jnp.sum)
                total = folded if total is None else total + folded
                out = nn_dot(kv[second, 1, k_band, span], weights.astype(jnp.bfloat16))
                blended = out if blended is None else blended + out
        m_later[...] = jnp.max(top, axis=0, keepdims=True)
        if now is not None:
            total = jnp.sum(total, axis=0, keepdims=True)
            lane = lax.broadcasted_iota(jnp.int32, (1, block), 1) + part * block
            mine = (lane >= first_len).astype(jnp.int32) == second
            o_buf[q_band, cols] = jnp.where(mine, blended * (1.0 / total), o_buf[q_band, cols])
            l_buf[head, :, cols] = jnp.where(mine, peak + jnp.log(total), l_buf[head, :, cols])

    def group(pair, outside):
        for head in range(per):
            second, part, cols, q_band, k_band, _ = place(pair * per + head, head)
            query = q_buf[q_band, cols]
            total = blended = None
            for start in range(0, keys, chunk):
                span = pl.ds(start, chunk)
                weights = jnp.exp(tn_dot(kv[second, 0, k_band, span], query))
                folded = fold(weights, jnp.sum)
                total = folded if total is None else total + folded
                out = nn_dot(kv[second, 1, k_band, span], weights.astype(jnp.bfloat16))
                blended = out if blended is None else blended + out
            total = jnp.sum(total, axis=0, keepdims=True)
            lane = lax.broadcasted_iota(jnp.int32, (1, block), 1) + part * block
            mine = (lane >= first_len).astype(jnp.int32) == second
            o_buf[q_band, cols] = jnp.where(mine, blended * (1.0 / total), o_buf[q_band, cols])
            l_buf[head, :, cols] = jnp.where(mine, jnp.log(total), l_buf[head, :, cols])
            inside_range = (total > 1e-20) & (total < 1e20)
            outside = jnp.maximum(outside, jnp.where(inside_range | ~mine, 0.0, 1.0))
        return outside

    outside = lax.fori_loop(0, pairs, group, jnp.zeros((1, block), jnp.float32))

    def two(index, carry):
        task = 2 * index
        step(task, task + 1, s_a, m_a, s_b, m_b)
        step(task + 1, jnp.minimum(task + 2, pairs * per - 1), s_b, m_b, s_a, m_a)
        return carry

    @pl.when(jnp.max(outside) > 0.0)
    def _():
        step(None, 0, None, None, s_a, m_a)
        lax.fori_loop(0, pairs * heads, two, 0)

    own_out[...] = o_buf[:columns]
    other_out[:columns] = o_buf[columns:].astype(jnp.bfloat16)
    for head in range(heads):
        own_lse[head : head + 1] = l_buf[head]
    rest = jnp.concatenate([l_buf[heads + head] for head in range(heads)] + [jnp.zeros((8 - heads, rows), jnp.float32)])
    terms = []
    for _ in range(3):
        terms.append(rest.astype(jnp.bfloat16).astype(jnp.float32))
        rest = rest - terms[-1]
    terms.append(jnp.zeros_like(rest))
    other_out[columns:] = jnp.concatenate(terms).astype(jnp.bfloat16)


def prefix_attend(owners, groups, lengths, me, own_q, other_q, units):
    columns, rows = own_q.shape
    share = units[0].shape[2]
    block = 256
    vmem = pl.BlockSpec(memory_space=pltpu.VMEM)
    out = jax.ShapeDtypeStruct((columns, rows), jnp.float32)
    lse = jax.ShapeDtypeStruct((8, rows), jnp.float32)
    sent = jax.ShapeDtypeStruct((columns + 32, rows), jnp.bfloat16)
    return pl.pallas_call(
        functools.partial(prefix_kernel, block, 256, len(units) - 1),
        out_shape=(out, lse, sent),
        in_specs=[pl.BlockSpec(memory_space=pltpu.SMEM)] * 4
        + [vmem] * 2
        + [pl.BlockSpec(memory_space=pl.ANY)] * len(units),
        out_specs=[vmem] * 3,
        scratch_shapes=[
            pltpu.VMEM((2, 2, columns, 2 * share), jnp.bfloat16),
            pltpu.VMEM((2 * columns, rows), jnp.bfloat16),
            pltpu.VMEM((2 * columns, rows), jnp.float32),
            pltpu.VMEM((16, 1, rows), jnp.float32),
            pltpu.VMEM((2 * share, block), jnp.float32),
            pltpu.VMEM((2 * share, block), jnp.float32),
            pltpu.VMEM((1, block), jnp.float32),
            pltpu.VMEM((1, block), jnp.float32),
            pltpu.SemaphoreType.DMA((4,)),
        ],
        cost_estimate=pl.CostEstimate(
            flops=32 * columns * rows * share, bytes_accessed=6 << 20, transcendentals=20 * rows * share
        ),
        name="prefix_attend",
    )(owners, groups, lengths, me, own_q, other_q, *units)


def merge_kernel(own_ref, own_lse_ref, got_ref, suffix_ref, suffix_lse_ref, out_ref):
    columns = own_ref.shape[0]
    packed = got_ref[columns:].astype(jnp.float32)
    got_lse = packed[:8] + packed[8:16] + packed[16:24]
    lses = [own_lse_ref[...], got_lse, suffix_lse_ref[...]]
    for head in range(columns // HEAD_SIZE):
        band = pl.ds(head * HEAD_SIZE, HEAD_SIZE)
        parts = [lse[head : head + 1] for lse in lses]
        top = jnp.maximum(jnp.maximum(parts[0], parts[1]), parts[2])
        factors = [jnp.exp(part - top) for part in parts]
        share = 1.0 / (factors[0] + factors[1] + factors[2])
        out_ref[band] = (
            own_ref[band] * (factors[0] * share)
            + got_ref[band].astype(jnp.float32) * (factors[1] * share)
            + suffix_ref[band] * (factors[2] * share)
        ).astype(jnp.bfloat16)


def merge(own, own_lse, got, suffix, suffix_lse):
    columns, rows = own.shape
    return pl.pallas_call(
        merge_kernel,
        out_shape=jax.ShapeDtypeStruct((columns, rows), jnp.bfloat16),
        grid=(rows // 256,),
        in_specs=[
            pl.BlockSpec((columns, 256), lambda i: (0, i)),
            pl.BlockSpec((8, 256), lambda i: (0, i)),
            pl.BlockSpec((columns + 32, 256), lambda i: (0, i)),
            pl.BlockSpec((columns, 256), lambda i: (0, i)),
            pl.BlockSpec((8, 256), lambda i: (0, i)),
        ],
        out_specs=pl.BlockSpec((columns, 256), lambda i: (0, i)),
        cost_estimate=pl.CostEstimate(flops=8 * columns * rows, bytes_accessed=1 << 20, transcendentals=15 * rows),
        name="merge",
    )(own, own_lse, got, suffix, suffix_lse)


def local(
    n_req,
    tokens,
    owners,
    request_groups,
    request_lengths,
    prefix_cache,
    attn_gain,
    query_weight,
    key_value_weight,
    query_gain,
    key_gain,
    w_out,
    ffn_gain,
    w_gate_up,
    w_down,
):
    row_count, width = tokens.shape
    columns = query_weight.shape[1]
    head_count = columns // HEAD_SIZE
    rank = lax.axis_index("tp")
    my_req = lax.axis_index("req")
    core = rank % 2

    def across_chip(value):
        return lax.ppermute(value, "tp", [(i, i ^ 2) for i in range(4)])

    def across_core(value):
        return lax.ppermute(value, "tp", [(i, i ^ 1) for i in range(4)])

    row_index = jnp.arange(row_count, dtype=jnp.int32)
    first_len = request_lengths[0, 0]
    segment = (row_index >= first_len).astype(jnp.int32)
    position = row_index - segment * first_len + PREFIX
    cos_part, sin_part = turns(position, HEAD_SIZE // 2)

    length = n_req // 2
    share = prefix_cache.shape[2] // 2
    mine = lax.dynamic_slice(jnp.transpose(prefix_cache[0], (0, 2, 1)), (0, 0, core * share), (2, columns, share))

    def ring(value):
        order = [*range(0, length, 2), *range(length - 1 - length % 2, 0, -2)]
        steps = zip(order, order[1:] + order[:1])
        return lax.ppermute(value, "req", [(2 * a + b, 2 * c + b) for a, c in steps for b in range(2)])

    def aside(value):
        return lax.ppermute(value, "req", [(r, r ^ 1) for r in range(n_req)])

    held = [mine, ring(mine)]
    units = [mine, aside(mine)]
    from_chip = across_chip(tokens)
    from_core = across_core(tokens)
    held[1], cos_part, sin_part = lax.optimization_barrier((held[1], cos_part, sin_part))
    from_chip, units[1], _ = lax.optimization_barrier((from_chip, units[1], held[1]))
    from_both = across_core(from_chip)
    full_rows, normalized_input = gather_norm(rank, (tokens, from_core, from_chip, from_both), attn_gain)

    w_out_held, _ = lax.optimization_barrier((w_out, from_chip))
    w_out_chip = across_chip(w_out_held)
    w_out_both = across_core(w_out_chip)

    query_rows = jnp.dot(
        normalized_input, query_weight, preferred_element_type=jnp.float32
    ).reshape(row_count, head_count, HEAD_SIZE)
    key_value_rows = jnp.dot(
        normalized_input, key_value_weight, preferred_element_type=jnp.float32
    ).reshape(row_count, 2, head_count, HEAD_SIZE)
    query_rows, key_value_rows, second = lax.optimization_barrier((query_rows, key_value_rows, ring(held[1])))
    units += [held[1], aside(held[1])]
    held.append(second)
    w_out_held, _ = lax.optimization_barrier((w_out, second))
    w_out_core = across_core(w_out_held)
    for _ in range(3, length):
        units += [held[-1], aside(held[-1])]
        held.append(ring(held[-1]))
    query_rows = rotate(rms_scale(query_rows, query_gain), cos_part, sin_part).astype(jnp.bfloat16)
    key_rows = rotate(rms_scale(key_value_rows[:, 0], key_gain), cos_part, sin_part).astype(jnp.bfloat16)
    value_rows = key_value_rows[:, 1].astype(jnp.bfloat16)
    cache_rows = jnp.stack(
        [key_rows.reshape(row_count, columns), value_rows.reshape(row_count, columns)],
        axis=1,
    )
    own_q = (query_rows * HEAD_SIZE**-0.5).reshape(row_count, columns).T
    other_q = across_core(own_q)
    suffix_out, suffix_lse = suffix_attend(
        request_lengths, own_q, key_rows.reshape(row_count, columns).T, value_rows.reshape(row_count, columns).T
    )

    held[-1], suffix_out, suffix_lse = lax.optimization_barrier((held[-1], suffix_out, suffix_lse))
    units += [held[-1], aside(held[-1][:1]), ring(units[-1][1:])]
    w_down_held, _ = lax.optimization_barrier((w_down, held[-1]))
    down_blocks = [
        lax.dynamic_slice_in_dim(w_down_held, (rank ^ flip) * width, width, 1) for flip in range(4)
    ]
    own_q, down_blocks = lax.optimization_barrier((own_q, down_blocks))
    own_out, own_lse, sent = prefix_attend(
        owners, request_groups, request_lengths, my_req.reshape(1), own_q, other_q, units
    )
    attention = merge(own_out, own_lse, across_core(sent), suffix_out, suffix_lse)
    att_chip = across_chip(attention)
    att_core = across_core(attention)
    near_total = full_rows.astype(jnp.float32) + tn_dot(attention, w_out) + tn_dot(att_core, w_out_core)
    near_total, att_chip = lax.optimization_barrier((near_total, att_chip))
    att_both = across_core(att_chip)
    mixed = near_total + tn_dot(att_chip, w_out_chip) + tn_dot(att_both, w_out_both)
    normed_ffn = rms_scale(mixed, ffn_gain).astype(jnp.bfloat16)
    gate_up = jnp.einsum("rd,dgf->rgf", normed_ffn, w_gate_up, preferred_element_type=jnp.float32)
    activated = (jax.nn.silu(gate_up[:, 0]) * gate_up[:, 1]).astype(jnp.bfloat16)

    def down(flip, rows=slice(None)):
        return jnp.dot(activated[rows], down_blocks[flip], preferred_element_type=jnp.float32).astype(jnp.bfloat16)

    first, second = slice(0, row_count // 2), slice(row_count // 2, row_count)
    got_first, far_second, near = lax.optimization_barrier(
        (across_core(down(3, first)), down(3, second), down(1))
    )
    sum_first = (down(2, first).astype(jnp.float32) + got_first.astype(jnp.float32)).astype(jnp.bfloat16)
    sum_first, got_second = lax.optimization_barrier((sum_first, across_core(far_second)))
    from_first = across_chip(sum_first)
    sum_second = (down(2, second).astype(jnp.float32) + got_second.astype(jnp.float32)).astype(jnp.bfloat16)
    from_second = across_chip(sum_second)
    activated, sum_second = lax.optimization_barrier((activated, sum_second))
    own_mixed = lax.dynamic_slice_in_dim(mixed, rank * width, width, 1)
    near_sum = own_mixed + down(0).astype(jnp.float32) + across_core(near).astype(jnp.float32)
    near_sum, from_first = lax.optimization_barrier((near_sum, from_first))
    done = (near_sum[first] + from_first.astype(jnp.float32)).astype(jnp.bfloat16)
    hidden = jnp.pad(done, ((0, row_count // 2), (0, 0)))
    hidden, from_second = lax.optimization_barrier((hidden, from_second))
    last = (near_sum[second] + from_second.astype(jnp.float32)).astype(jnp.bfloat16)
    return (lax.dynamic_update_slice(hidden, last, (row_count // 2, 0)), cache_rows)


def solution(mesh):
    placed = (
        P("req", "tp"),
        P(),
        P("req", None),
        P("req", None),
        P("req", None, None, None),
        P(),
        P(None, "tp"),
        P(),
        P(),
        P(),
        P("tp", None),
        P(),
        P(None, None, "tp"),
        P("tp", None),
    )
    return jax.shard_map(
        functools.partial(local, mesh.shape["req"]),
        mesh=mesh,
        in_specs=placed,
        out_specs=(P("req", "tp"), P("req", None, None)),
        check_vma=False,
    )
```
